512 devices in a mesh: dp: 8 (over z_hi, core), seq: 64 (over z_lo, x, y).
Axes of the slice: x: 4, y: 8, z: 8 (z_hi: 4, z_lo: 2; z = z_hi * 2 + z_lo), core: 2. Of those that a mesh axis runs over, the one named last changes fastest.
Arguments:
- features: bfloat16 [8, 8192, 512], P('dp', 'seq'), may hold values from -40 to 40
- score_cotangent: float32 [8, 8192], P('dp', 'seq'), may hold values from -24 to 24
- projection_weight: bfloat16 [512, 768], replicated, may hold values from -0.25 to 0.25
- squeeze_weight: bfloat16 [64, 768], replicated, may hold values from -0.21875 to 0.21875
- first_weight: bfloat16 [320, 128], replicated, may hold values from -0.3125 to 0.3125
- second_weight: bfloat16 [640, 256], replicated, may hold values from -0.25 to 0.25
- third_weight: bfloat16 [1280, 256], replicated, may hold values from -0.15625 to 0.15625
- final_weight: bfloat16 [768], replicated, may hold values from -0.875 to 0.875
Outputs:
- scores: float32 [8, 8192], P('dp', 'seq')
- feature_grad: float32 [8, 8192, 512], P('dp', 'seq')
- squeeze_grad: float32 [64, 768], P('seq')
- first_grad: float32 [320, 128], P('seq')
- second_grad: float32 [640, 256], P('seq')
- third_grad: float32 [1280, 256], P('seq')
- final_grad: float32 [768], P('seq')
The draws below stay inside these ranges and needn't reach their ends.
All inputs are finite; a program needn't handle non-finite values.
Results may differ from the reference program's by a relative error of at most 0.025.
Values may be sent and summed in bfloat16 or wider, within the bound.
A program may use at most 64 MiB of HBM per device.

```python
import math
import jax
import jax.numpy as jnp
from jax import lax

D = 768
FEAT = 512
C0 = 64
C1 = 128
C2 = 256
HK = 5
PK = 3
FRAMES = 8192
UTTS = 8


def draw_features(key, part):
    noise_key, row_key, column_key = jax.random.split(key, 3)
    array_shape = (UTTS, FRAMES, FEAT)
    base_values = jnp.clip(jax.random.normal(noise_key, array_shape, jnp.float32), -4.0, 4.0)
    row_scale = jnp.exp(jax.random.uniform(row_key, (UTTS, FRAMES, 1), jnp.float32, math.log(0.3), math.log(3.0)))
    columns = jnp.exp(jax.random.uniform(column_key, (1, 1, FEAT), jnp.float32, math.log(0.3), math.log(3.0)))
    values = base_values * row_scale * columns
    return values.astype(jnp.bfloat16)


def level_of(key, extent, cuts, low, high):
    gain = 1.0
    for dim, parts in cuts:
        draws = jax.random.uniform(jax.random.fold_in(jax.random.fold_in(key, 6), dim), (parts,), jnp.float32, low / len(cuts), high / len(cuts))
        gain = gain * jnp.repeat(jnp.exp(draws), extent[dim] // parts).reshape((-1,) + (1,) * (len(extent) - 1 - dim))
    return gain


def bell_draw(key, extent, width, bound, cuts=(), held_as=jnp.bfloat16):
    result = width * jax.random.normal(key, extent, jnp.float32)
    if cuts:
        result = result * level_of(key, extent, cuts, -0.22, 0.18)
    return jnp.clip(result, -bound, bound).astype(held_as)


def setup_inputs(seed: int = 0) -> dict:
    keys = jax.random.split(jax.random.key(seed), 9)
    return {
        "features": draw_features(jax.random.fold_in(keys[8], 71), 0),
        "score_cotangent": bell_draw(keys[1], (UTTS, FRAMES), 4.0, 24.0, ((0, 8), (1, 64)), jnp.float32),
        "projection_weight": bell_draw(keys[2], (FEAT, D), FEAT ** -0.5, 0.25),
        "squeeze_weight": bell_draw(keys[3], (C0, D), D ** -0.5, 0.21875),
        "first_weight": bell_draw(keys[4], (HK * C0, C1), (HK * C0) ** -0.5, 0.3125),
        "second_weight": bell_draw(keys[5], (HK * C1, C2), (HK * C1) ** -0.5, 0.25),
        "third_weight": bell_draw(keys[6], (HK * C2, C2), (HK * C2) ** -0.5, 0.15625),
        "final_weight": bell_draw(keys[7], (PK * C2,), (PK * C2 // 16) ** -0.5, 0.875),
    }


EPSILON = 1e-05
SLOPE = 0.1

def normalize(values):
    average = lax.optimization_barrier(jnp.mean(values, axis=-1, keepdims=True))
    centred = values - average
    variance = lax.optimization_barrier(jnp.mean(centred * centred, axis=-1, keepdims=True))
    inverse = lax.rsqrt(variance + EPSILON)
    return (centred * inverse, inverse)

def normalize_back(upstream, normed, inverse):
    first_mean = lax.optimization_barrier(jnp.mean(upstream, axis=-1, keepdims=True))
    second_mean = lax.optimization_barrier(jnp.mean(upstream * normed, axis=-1, keepdims=True))
    return (upstream - first_mean - normed * second_mean) * inverse

def gelu_slope(values):
    cumulative = 0.5 * (1.0 + lax.erf(values * math.sqrt(0.5)))
    density = jnp.exp(-0.5 * values * values) / math.sqrt(2.0 * math.pi)
    return cumulative + values * density

def leaky_unit(values):
    return SLOPE * values + (1.0 - SLOPE) * jax.nn.gelu(values, approximate=False)

def leaky_slope(values):
    return SLOPE + (1.0 - SLOPE) * gelu_slope(values)

def convolve(extended, weights):
    return lax.conv_general_dilated(extended, weights, (1,), 'VALID', dimension_numbers=('NWC', 'WIO', 'NWC'), preferred_element_type=jnp.float32)

def flipped_plain(weights):
    return jnp.swapaxes(weights, 1, 2)[::-1]

def tap_gradients(extended, delta, tap_count):
    length = delta.shape[0]
    pieces = [jnp.dot(extended[offset:offset + length].T, delta, preferred_element_type=jnp.float32) for offset in range(tap_count)]
    return jnp.concatenate(pieces, axis=0)

def reference(features, score_cotangent, projection_weight, squeeze_weight, first_weight, second_weight, third_weight, final_weight):
    kernels = [first_weight.reshape(HK, C0, C1), second_weight.reshape(HK, C1, C2), third_weight.reshape(HK, C2, C2)]
    final_kernel = final_weight.reshape(PK, C2, 1)
    final_taps = final_weight.astype(jnp.float32).reshape(PK, C2)
    head_pad = (HK - 1) // 2
    final_pad = (PK - 1) // 2

    def single(inputs):
        feature_rows, cotangent = inputs
        frames = cotangent.shape[0]
        normed_in, inverse_in = normalize(feature_rows.astype(jnp.float32))
        rounded_in = normed_in.astype(jnp.bfloat16)
        projected = jnp.dot(rounded_in, projection_weight, preferred_element_type=jnp.float32).astype(jnp.bfloat16)
        hidden_normed, hidden_inverse = normalize(projected.astype(jnp.float32))
        hidden = hidden_normed.astype(jnp.bfloat16)
        squeezed = lax.dot_general(hidden, squeeze_weight, (((1,), (1,)), ((), ())), preferred_element_type=jnp.float32)
        layer_input = leaky_unit(squeezed).astype(jnp.bfloat16)
        extended_list = []
        action_list = []
        for kernel in kernels:
            extended = jnp.pad(layer_input, ((head_pad, head_pad), (0, 0)))
            action = convolve(extended[None], kernel)[0]
            extended_list.append(extended)
            action_list.append(action)
            layer_input = leaky_unit(action).astype(jnp.bfloat16)
        final_ext = jnp.pad(layer_input, ((final_pad, final_pad), (0, 0)))
        scores = convolve(final_ext[None], final_kernel)[0, :, 0]
        cotangent_ext = jnp.pad(cotangent, (final_pad, final_pad))
        upstream = jnp.zeros((frames, C2), jnp.float32)
        for offset in range(PK):
            upstream = upstream + cotangent_ext[offset:offset + frames, None] * final_taps[PK - 1 - offset][None, :]
        final_grad = jnp.concatenate([jnp.dot(cotangent, final_ext[offset:offset + frames].astype(jnp.float32), precision=lax.Precision.HIGHEST) for offset in range(PK)], axis=0)
        layer_grads = [None, None, None]
        for layer_index in (2, 1, 0):
            delta = (upstream * leaky_slope(action_list[layer_index])).astype(jnp.bfloat16)
            layer_grads[layer_index] = tap_gradients(extended_list[layer_index], delta, HK)
            delta_ext = jnp.pad(delta, ((head_pad, head_pad), (0, 0)))
            upstream = convolve(delta_ext[None], flipped_plain(kernels[layer_index]))[0]
        delta_squeeze = (upstream * leaky_slope(squeezed)).astype(jnp.bfloat16)
        squeeze_grad = jnp.dot(delta_squeeze.T, hidden, preferred_element_type=jnp.float32)
        hidden_upstream = jnp.dot(delta_squeeze, squeeze_weight, preferred_element_type=jnp.float32)
        projected_grad = normalize_back(hidden_upstream, hidden_normed, hidden_inverse).astype(jnp.bfloat16)
        normed_grad = lax.dot_general(projected_grad, projection_weight, (((1,), (1,)), ((), ())), preferred_element_type=jnp.float32)
        feature_grad = normalize_back(normed_grad, normed_in, inverse_in)
        return (scores, feature_grad, squeeze_grad, layer_grads[0], layer_grads[1], layer_grads[2], final_grad)
    results = lax.map(single, (features, score_cotangent))
    factor = 1.0 / math.sqrt(UTTS * FRAMES)
    return (results[0], results[1], lax.optimization_barrier(jnp.sum(results[2], axis=0)) * factor, lax.optimization_barrier(jnp.sum(results[3], axis=0)) * factor, lax.optimization_barrier(jnp.sum(results[4], axis=0)) * factor, lax.optimization_barrier(jnp.sum(results[5], axis=0)) * factor, lax.optimization_barrier(jnp.sum(results[6], axis=0)) * factor)
```

```python
import math

import jax
import jax.numpy as jnp
from jax import lax
from jax.experimental import pallas as pl
from jax.experimental.pallas import tpu as pltpu
from jax.sharding import PartitionSpec as P

MESH = pl.DeviceIdType.MESH
F32 = jnp.float32
BF16 = jnp.bfloat16

C0, C1, C2 = 64, 128, 256
HK, PK = 5, 3
EPSILON = 1e-05
SLOPE = 0.1
FRAMES = 128
HALO = 16
ROWS = FRAMES + 2 * HALO
OWN = slice(HALO, HALO + FRAMES)

ZH, CORES, ZL, NX, NY = 4, 2, 2, 4, 8
NZ = ZH * ZL
SHARES = ZL * NX * NY
TROWS, RROWS = 24, 16


def dot(a, b, ca=1, cb=0):
    return lax.dot_general(a, b, (((ca,), (cb,)), ((), ())), preferred_element_type=F32)


def normalize(values):
    average = jnp.mean(values, axis=-1, keepdims=True)
    centred = values - average
    variance = jnp.mean(centred * centred, axis=-1, keepdims=True)
    inverse = lax.rsqrt(variance + EPSILON)
    return centred * inverse, inverse


def normalize_back(upstream, normed, inverse):
    first_mean = jnp.mean(upstream, axis=-1, keepdims=True)
    second_mean = jnp.mean(upstream * normed, axis=-1, keepdims=True)
    return (upstream - first_mean - normed * second_mean) * inverse


def activation(v):
    cumulative = 0.5 * (1.0 + lax.erf(v * math.sqrt(0.5)))
    density = jnp.exp(-0.5 * v * v) * (1.0 / math.sqrt(2.0 * math.pi))
    value = SLOPE * v + (1.0 - SLOPE) * (v * cumulative)
    slope = SLOPE + (1.0 - SLOPE) * (cumulative + v * density)
    return value, slope


def shifted(v, shift):
    return pltpu.roll(v, (-shift) % v.shape[0], 0) if shift else v


def split3(v):
    hi = v.astype(BF16).astype(F32)
    mid = (v - hi).astype(BF16).astype(F32)
    return hi, mid, (v - hi - mid).astype(BF16).astype(F32)


def kernel(
    feat, cot, wp, ws, w1, w2, w3, wf,
    scores, fgrad, sq_out, g1_out, g2_out, g3_out, gf_out,
    hfeat, hcot, xr, x2, x3, cots, wfs, g3s, g2s, g1s, tst, rst,
    tb, rb, t0, r0, t1, r1, tx, ry, t2, r2, ty, rx, zs, zr, fin,
    hs, hr, s0, q0, sx, qx, sy, qy, sy2, qy2, sx2, qx2, sz, qz, s4, q4,
):
    dp, sq = lax.axis_index("dp"), lax.axis_index("seq")
    zh, core = dp // CORES, dp % CORES
    zl, px, py = sq // (NX * NY), (sq // NY) % NX, sq % NY
    pz = zh * ZL + zl
    count = SHARES

    def at(z=None, x=None, y=None, c=None):
        z = pz if z is None else z
        x = px if x is None else x
        y = py if y is None else y
        c = core if c is None else c
        return ((z // ZL) * CORES + c, (z % ZL) * NX * NY + x * NY + y)

    before = (dp, (sq + count - 1) % count)
    after = (dp, (sq + 1) % count)
    partner = at(c=1 - core)
    peers = [before, after, partner]
    peers += [at(x=(px + d) % NX) for d in range(1, NX)]
    peers += [at(y=(py + d) % NY) for d in range(1, NY)]
    peers += [at(z=(pz + d) % NZ) for d in range(1, NZ)]

    barrier = pltpu.get_barrier_semaphore()
    for peer in peers:
        pl.semaphore_signal(barrier, inc=1, device_id=peer, device_id_type=MESH)
    pl.semaphore_wait(barrier, len(peers))

    def send(src, dst, ss, rs, peer):
        copy = pltpu.make_async_remote_copy(
            src_ref=src, dst_ref=dst, send_sem=ss, recv_sem=rs, device_id=peer, device_id_type=MESH
        )
        copy.start()
        return copy

    halo = [
        send(feat.at[0, pl.ds(FRAMES - HALO, HALO)], hfeat.at[0], hs.at[0], hr.at[0], after),
        send(feat.at[0, pl.ds(0, HALO)], hfeat.at[1], hs.at[1], hr.at[1], before),
        send(cot, hcot.at[0], hs.at[2], hr.at[2], after),
        send(cot, hcot.at[1], hs.at[3], hr.at[3], before),
    ]

    has_low, has_high = sq > 0, sq < count - 1
    row = lax.broadcasted_iota(jnp.int32, (ROWS, 1), 0)
    first_row = jnp.where(has_low, 0, HALO)
    last_row = jnp.where(has_high, ROWS, HALO + FRAMES)
    inside = jnp.logical_and(row >= first_row, row < last_row)

    def masked(v):
        return jnp.where(inside, v, 0.0)

    normed_in, inverse_in = normalize(feat[0].astype(F32))
    xr[OWN] = normed_in.astype(BF16)
    for copy in halo:
        copy.wait()
    edge = jnp.concatenate(
        [
            jnp.where(has_low, hfeat[0].astype(F32), 0.0),
            jnp.where(has_high, hfeat[1].astype(F32), 0.0),
        ],
        axis=0,
    )
    edge = normalize(edge)[0].astype(BF16)
    xr[0:HALO] = edge[0:HALO]
    xr[HALO + FRAMES : ROWS] = edge[HALO:]

    projected = dot(xr[...], wp[...]).astype(BF16)
    hidden_all, hidden_inverse = normalize(projected.astype(F32))
    hidden = hidden_all.astype(BF16)
    hidden_normed, hidden_inverse = hidden_all[OWN], hidden_inverse[OWN]
    squeezed = dot(hidden, ws[...], 1, 1)
    hidden = hidden[OWN]

    v1, squeezed_slope = activation(squeezed)
    v1 = v1.astype(BF16).astype(F32)
    taps1 = [shifted(v1, k - 2).astype(BF16) for k in range(HK)]
    first_act = sum(dot(taps1[k], w1[k * C0 : (k + 1) * C0]) for k in range(HK))

    v2, slope1 = activation(first_act)
    v2 = masked(v2)
    for k in range(HK):
        x2[:, k * C1 : (k + 1) * C1] = shifted(v2, k - 2).astype(BF16)
    second_act = dot(x2[...], w2[...])

    v3, slope2 = activation(second_act)
    v3 = masked(v3)
    for k in range(HK):
        x3[:, k * C2 : (k + 1) * C2] = shifted(v3, k - 2).astype(BF16)
    third_act = dot(x3[...], w3[...])

    v4, slope3 = activation(third_act)
    v4 = masked(v4)
    final_taps = [shifted(v4, k - 1)[OWN].astype(BF16) for k in range(PK)]
    wrow = [wf[k : k + 1, :] for k in range(PK)]
    total = sum(dot(jnp.broadcast_to(wrow[k], (8, C2)), final_taps[k], 1, 1) for k in range(PK))
    scores[...] = total[0:1]

    low = jnp.where(has_low, hcot[0], 0.0)
    high = jnp.where(has_high, hcot[1], 0.0)
    line = jnp.concatenate([low, cot[...], high], axis=1)
    cots[...] = jnp.zeros_like(cots)
    wfs[...] = jnp.zeros_like(wfs)
    pieces = split3(line)
    for p in range(3):
        for k in range(PK):
            start = FRAMES - HALO - k + 1
            cots[3 * k + p : 3 * k + p + 1, :] = pltpu.roll(pieces[p], 3 * FRAMES - start, 1)[:, : 2 * FRAMES]
            wfs[3 * k + p : 3 * k + p + 1, :] = wrow[k].astype(F32)
        cots[16 + p : 17 + p, 0:FRAMES] = pieces[p][:, FRAMES : 2 * FRAMES]
    upstream = dot(cots[0:16].astype(BF16), wfs[...].astype(BF16), 0, 0)[:ROWS]
    own_cot = cots[16:24, 0:FRAMES].astype(BF16)
    final_grad = [
        jnp.sum(dot(own_cot, final_taps[k]), axis=0, keepdims=True) for k in range(PK)
    ]

    delta = masked(upstream * slope3).astype(BF16)
    grad = dot(x3[OWN], delta[OWN], 0, 0)
    g3s[0], g3s[1] = grad[:, :128], grad[:, 128:]
    for h in range(CORES):
        for r in range(20):
            tst.at[h][pl.ds(r, SHARES, stride=TROWS), :] = g3s.at[h][pl.ds(r, SHARES, stride=20), :]
        for r in range(20, TROWS):
            tst.at[h][pl.ds(r, SHARES, stride=TROWS), :] = jnp.zeros((SHARES, 128), F32)
        for s in range(SHARES):
            a, b, c = s // (NX * NY), (s // NY) % NX, s % NY
            tb[h, b, c, a] = tst[h, s * TROWS : (s + 1) * TROWS].astype(BF16)
    core_t = send(tb.at[1 - core], t0, s0.at[0], q0.at[0], partner)

    def back(delta, weight, width):
        d = delta.astype(F32)
        return sum(
            dot(shifted(d, 2 - k).astype(BF16), weight[k * width : (k + 1) * width], 1, 1)
            for k in range(HK)
        )

    upstream = back(delta, w3, C2)
    delta = masked(upstream * slope2).astype(BF16)
    grad = dot(x2[OWN], delta[OWN], 0, 0)
    g2s[0], g2s[1] = grad[:, :128], grad[:, 128:]
    for h in range(CORES):
        for r in range(10):
            rst.at[h][pl.ds(r, SHARES, stride=RROWS), :] = g2s.at[h][pl.ds(r, SHARES, stride=10), :]

    upstream = back(delta, w2, C1)
    delta = masked(upstream * slope1).astype(BF16)
    for k in range(HK):
        g1s[k * C0 : (k + 1) * C0] = dot(taps1[k][OWN], delta[OWN], 0, 0)
    for r in range(5):
        rst.at[1][pl.ds(10 + r, SHARES, stride=RROWS), :] = g1s[pl.ds(r, SHARES, stride=5), :]

    flat = jnp.concatenate(final_grad, axis=1)
    width = (PK * C2) // SHARES
    offset = lax.broadcasted_iota(jnp.int32, (SHARES, PK * C2), 1) - width * lax.broadcasted_iota(
        jnp.int32, (SHARES, PK * C2), 0
    )
    picked = jnp.where(jnp.logical_and(offset >= 0, offset < width), flat, 0.0).astype(BF16)
    place = lax.broadcasted_iota(jnp.int32, (PK * C2, 128), 0)
    place = place - width * ((place * 5462) >> 16) - lax.broadcasted_iota(jnp.int32, (PK * C2, 128), 1)
    spread = jnp.where(place == 0, 1.0, 0.0).astype(BF16)
    rst.at[1][pl.ds(15, SHARES, stride=RROWS), :] = dot(picked, spread)

    upstream = back(delta, w1, C0)
    delta_squeeze = (upstream[OWN] * squeezed_slope[OWN]).astype(BF16)
    grad = dot(delta_squeeze, hidden, 0, 0)
    for j in range(6):
        rst.at[0][pl.ds(10 + j, SHARES, stride=RROWS), :] = grad[:, j * 128 : (j + 1) * 128]
    for h in range(CORES):
        for s in range(SHARES):
            a, b, c = s // (NX * NY), (s // NY) % NX, s % NY
            rb[h, c, b, a] = rst[h, s * RROWS : (s + 1) * RROWS].astype(BF16)
    core_r = send(rb.at[1 - core], r0, s0.at[1], q0.at[1], partner)

    core_t.wait()
    t1[...] = (tb[core].astype(F32) + t0[...].astype(F32)).astype(BF16)
    along_x = [
        send(t1.at[(px + d) % NX], tx.at[d - 1], sx.at[d - 1], qx.at[d - 1], at(x=(px + d) % NX))
        for d in range(1, NX)
    ]
    core_r.wait()
    r1[...] = (rb[core].astype(F32) + r0[...].astype(F32)).astype(BF16)
    along_y = [
        send(r1.at[(py + d) % NY], ry.at[d - 1], sy.at[d - 1], qy.at[d - 1], at(y=(py + d) % NY))
        for d in range(1, NY)
    ]

    hidden_upstream = dot(delta_squeeze, ws[...])
    projected_grad = normalize_back(hidden_upstream, hidden_normed, hidden_inverse).astype(BF16)
    normed_grad = dot(projected_grad, wp[...], 1, 1)
    fgrad[0] = normalize_back(normed_grad, normed_in, inverse_in)

    for copy in along_x:
        copy.wait()
    acc = t1[px].astype(F32)
    for d in range(NX - 1):
        acc = acc + tx[d].astype(F32)
    t2[...] = acc.astype(BF16)
    along_y2 = [
        send(t2.at[(py + d) % NY], ty.at[d - 1], sy2.at[d - 1], qy2.at[d - 1], at(y=(py + d) % NY))
        for d in range(1, NY)
    ]
    for copy in along_y:
        copy.wait()
    acc = r1[py].astype(F32)
    for d in range(NY - 1):
        acc = acc + ry[d].astype(F32)
    r2[...] = acc.astype(BF16)
    along_x2 = [
        send(r2.at[(px + d) % NX], rx.at[d - 1], sx2.at[d - 1], qx2.at[d - 1], at(x=(px + d) % NX))
        for d in range(1, NX)
    ]
    for copy in along_x2:
        copy.wait()
    acc = r2[px].astype(F32)
    for d in range(NX - 1):
        acc = acc + rx[d].astype(F32)
    zs[:, TROWS:] = acc.astype(BF16)
    for copy in along_y2:
        copy.wait()
    acc = t2[py].astype(F32)
    for d in range(NY - 1):
        acc = acc + ty[d].astype(F32)
    zs[:, :TROWS] = acc.astype(BF16)

    along_z = []
    for d in range(1, NZ):
        target = (pz + d) % NZ
        along_z.append(send(zs.at[target % ZL], zr.at[d], sz.at[d - 1], qz.at[d - 1], at(z=target)))
    for copy in along_z:
        copy.wait()
    zr[0] = zs[zl]
    acc = jnp.zeros((TROWS + RROWS, 128), F32)
    for z in range(NZ):
        acc = acc + zr[(pz + NZ - z) % NZ].astype(F32)
    fin[core] = acc * (1.0 / math.sqrt(FRAMES * SHARES * ZH * CORES))
    send(fin.at[core], fin.at[core], s4, q4, partner).wait()

    g3_out[...] = jnp.concatenate([fin[0, 0:20], fin[1, 0:20]], axis=1)
    g2_out[...] = jnp.concatenate([fin[0, 24:34], fin[1, 24:34]], axis=1)
    g1_out[...] = fin[1, 34:39]
    gf_out[...] = fin[1, 39:40]
    for j in range(6):
        sq_out[:, j * 128 : (j + 1) * 128] = fin[0, 34 + j : 35 + j]


def shards(features, cotangent, wp, ws, w1, w2, w3, wf):
    vmem = pl.BlockSpec(memory_space=pltpu.VMEM)
    dma = pltpu.SemaphoreType.DMA
    outs = pl.pallas_call(
        kernel,
        out_shape=(
            jax.ShapeDtypeStruct((1, FRAMES), F32),
            jax.ShapeDtypeStruct((1, FRAMES, 512), F32),
            jax.ShapeDtypeStruct((1, 768), F32),
            jax.ShapeDtypeStruct((5, 128), F32),
            jax.ShapeDtypeStruct((10, 256), F32),
            jax.ShapeDtypeStruct((20, 256), F32),
            jax.ShapeDtypeStruct((1, 128), F32),
        ),
        in_specs=[vmem] * 8,
        out_specs=(vmem,) * 7,
        scratch_shapes=[
            pltpu.VMEM((2, HALO, 512), BF16),
            pltpu.VMEM((2, 1, FRAMES), F32),
            pltpu.VMEM((ROWS, 512), BF16),
            pltpu.VMEM((ROWS, HK * C1), BF16),
            pltpu.VMEM((ROWS, HK * C2), BF16),
            pltpu.VMEM((24, 2 * FRAMES), F32),
            pltpu.VMEM((16, C2), F32),
            pltpu.VMEM((2, HK * C2, 128), F32),
            pltpu.VMEM((2, HK * C1, 128), F32),
            pltpu.VMEM((HK * C0, 128), F32),
            pltpu.VMEM((2, SHARES * TROWS, 128), F32),
            pltpu.VMEM((2, SHARES * RROWS, 128), F32),
            pltpu.VMEM((2, NX, NY, ZL, TROWS, 128), BF16),
            pltpu.VMEM((2, NY, NX, ZL, RROWS, 128), BF16),
            pltpu.VMEM((NX, NY, ZL, TROWS, 128), BF16),
            pltpu.VMEM((NY, NX, ZL, RROWS, 128), BF16),
            pltpu.VMEM((NX, NY, ZL, TROWS, 128), BF16),
            pltpu.VMEM((NY, NX, ZL, RROWS, 128), BF16),
            pltpu.VMEM((NX - 1, NY, ZL, TROWS, 128), BF16),
            pltpu.VMEM((NY - 1, NX, ZL, RROWS, 128), BF16),
            pltpu.VMEM((NY, ZL, TROWS, 128), BF16),
            pltpu.VMEM((NX, ZL, RROWS, 128), BF16),
            pltpu.VMEM((NY - 1, ZL, TROWS, 128), BF16),
            pltpu.VMEM((NX - 1, ZL, RROWS, 128), BF16),
            pltpu.VMEM((ZL, TROWS + RROWS, 128), BF16),
            pltpu.VMEM((NZ, TROWS + RROWS, 128), BF16),
            pltpu.VMEM((2, TROWS + RROWS, 128), F32),
            dma((4,)), dma((4,)),
            dma((2,)), dma((2,)),
            dma((NX - 1,)), dma((NX - 1,)),
            dma((NY - 1,)), dma((NY - 1,)),
            dma((NY - 1,)), dma((NY - 1,)),
            dma((NX - 1,)), dma((NX - 1,)),
            dma((NZ - 1,)), dma((NZ - 1,)),
            dma, dma,
        ],
        compiler_params=pltpu.CompilerParams(collective_id=0, has_side_effects=True),
    )(features, cotangent, wp, ws, w1, w2, w3, wf.reshape(PK, C2))
    scores, fgrad, sq, g1, g2, g3, gf = outs
    return scores, fgrad, sq, g1, g2, g3, gf[0, : (PK * C2) // SHARES]


def solution(mesh):
    placed = (P("dp", "seq", None), P("dp", "seq"), P(), P(), P(), P(), P(), P())
    return jax.shard_map(
        shards,
        mesh=mesh,
        in_specs=placed,
        out_specs=(
            P("dp", "seq"),
            P("dp", "seq", None),
            P("seq", None),
            P("seq", None),
            P("seq", None),
            P("seq", None),
            P("seq"),
        ),
        check_vma=False,
    )
```

```python
import math

import jax
import jax.numpy as jnp
from jax import lax
from jax.experimental import pallas as pl
from jax.experimental.pallas import tpu as pltpu
from jax.sharding import PartitionSpec as P

MESH = pl.DeviceIdType.MESH
F32 = jnp.float32
BF16 = jnp.bfloat16

C0, C1, C2 = 64, 128, 256
HK, PK = 5, 3
EPSILON = 1e-05
SLOPE = 0.1
FRAMES = 128
HALO = 16
ROWS = FRAMES + 2 * HALO
OWN = slice(HALO, HALO + FRAMES)

ZH, CORES, ZL, NX, NY = 4, 2, 2, 4, 8
NZ = ZH * ZL
SHARES = ZL * NX * NY
TROWS, RROWS = 24, 16


def dot(a, b, ca=1, cb=0):
    return lax.dot_general(a, b, (((ca,), (cb,)), ((), ())), preferred_element_type=F32)


def normalize(values):
    average = jnp.mean(values, axis=-1, keepdims=True)
    centred = values - average
    variance = jnp.mean(centred * centred, axis=-1, keepdims=True)
    inverse = lax.rsqrt(variance + EPSILON)
    return centred * inverse, inverse


def normalize_back(upstream, normed, inverse):
    first_mean = jnp.mean(upstream, axis=-1, keepdims=True)
    second_mean = jnp.mean(upstream * normed, axis=-1, keepdims=True)
    return (upstream - first_mean - normed * second_mean) * inverse


def activation(v):
    cumulative = 0.5 * (1.0 + lax.erf(v * math.sqrt(0.5)))
    density = jnp.exp(-0.5 * v * v) * (1.0 / math.sqrt(2.0 * math.pi))
    value = SLOPE * v + (1.0 - SLOPE) * (v * cumulative)
    slope = SLOPE + (1.0 - SLOPE) * (cumulative + v * density)
    return value, slope


def shifted(v, shift):
    return pltpu.roll(v, (-shift) % v.shape[0], 0) if shift else v


def split3(v):
    hi = v.astype(BF16).astype(F32)
    mid = (v - hi).astype(BF16).astype(F32)
    return hi, mid, (v - hi - mid).astype(BF16).astype(F32)


def kernel(
    feat_in, cot_in, wp_in, ws_in, w1_in, w2_in, w3_in, wf_in,
    scores, fgrad, fin_out,
    feat, cot, wp, ws, w1, w2, w3, wf, in_sem,
    hfeat, hcot, x2, x3, cots, wfs, g3s, g2s, g1s, tst, rst,
    tb, rb, t0, r0, t1, r1, tx, ry, t2, r2, ty, rx, zs, zr, fin,
    hs, hr, s0, q0, sx, qx, sy, qy, sy2, qy2, sx2, qx2, sz, qz, s4, q4,
):
    dp, sq = lax.axis_index("dp"), lax.axis_index("seq")
    zh, core = dp // CORES, dp % CORES
    zl, px, py = sq // (NX * NY), (sq // NY) % NX, sq % NY
    pz = zh * ZL + zl
    count = SHARES

    def at(z=None, x=None, y=None, c=None):
        z = pz if z is None else z
        x = px if x is None else x
        y = py if y is None else y
        c = core if c is None else c
        return ((z // ZL) * CORES + c, (z % ZL) * NX * NY + x * NY + y)

    before = (dp, (sq + count - 1) % count)
    after = (dp, (sq + 1) % count)
    partner = at(c=1 - core)
    peers = [before, after, partner]
    peers += [at(x=(px + d) % NX) for d in range(1, NX)]
    peers += [at(y=(py + d) % NY) for d in range(1, NY)]
    peers += [at(z=(pz + d) % NZ) for d in range(1, NZ)]

    barrier = pltpu.get_barrier_semaphore()
    for peer in peers:
        pl.semaphore_signal(barrier, inc=1, device_id=peer, device_id_type=MESH)
    sources = (feat_in.at[0], cot_in, wp_in, ws_in, w1_in, w2_in, w3_in, wf_in)
    loads = [
        pltpu.make_async_copy(source, target, in_sem.at[i])
        for i, (source, target) in enumerate(zip(sources, (feat, cot, wp, ws, w1, w2, w3, wf)))
    ]
    for load in loads:
        load.start()
    pl.semaphore_wait(barrier, len(peers))

    def send(src, dst, ss, rs, peer):
        copy = pltpu.make_async_remote_copy(
            src_ref=src, dst_ref=dst, send_sem=ss, recv_sem=rs, device_id=peer, device_id_type=MESH
        )
        copy.start()
        return copy

    halo = [
        send(feat_in.at[0, pl.ds(FRAMES - HALO, HALO)], hfeat.at[0], hs.at[0], hr.at[0], after),
        send(feat_in.at[0, pl.ds(0, HALO)], hfeat.at[1], hs.at[1], hr.at[1], before),
        send(cot_in, hcot.at[0], hs.at[2], hr.at[2], after),
        send(cot_in, hcot.at[1], hs.at[3], hr.at[3], before),
    ]

    has_low, has_high = sq > 0, sq < count - 1
    row = lax.broadcasted_iota(jnp.int32, (ROWS, 1), 0)
    first_row = jnp.where(has_low, 0, HALO)
    last_row = jnp.where(has_high, ROWS, HALO + FRAMES)
    inside = jnp.logical_and(row >= first_row, row < last_row)

    def masked(v):
        return jnp.where(inside, v, 0.0)

    def front(rounded):
        projected = dot(rounded, wp[...]).astype(BF16)
        normed, inverse = normalize(projected.astype(F32))
        rounded = normed.astype(BF16)
        return normed, inverse, rounded, dot(rounded, ws[...], 1, 1)

    loads[0].wait()
    normed_in, inverse_in = normalize(feat[...].astype(F32))
    loads[2].wait()
    loads[3].wait()
    hidden_normed, hidden_inverse, hidden, squeezed = front(normed_in.astype(BF16))
    for i in (1, 4, 5, 6, 7):
        loads[i].wait()
    for copy in halo:
        copy.wait()
    edge = jnp.concatenate(
        [
            jnp.where(has_low, hfeat[0].astype(F32), 0.0),
            jnp.where(has_high, hfeat[1].astype(F32), 0.0),
        ],
        axis=0,
    )
    edge = front(normalize(edge)[0].astype(BF16))[3]
    squeezed = jnp.concatenate([edge[:HALO], squeezed, edge[HALO:]], axis=0)

    v1, squeezed_slope = activation(squeezed)
    v1 = v1.astype(BF16).astype(F32)
    taps1 = [shifted(v1, k - 2).astype(BF16) for k in range(HK)]
    first_act = sum(dot(taps1[k], w1[k * C0 : (k + 1) * C0]) for k in range(HK))

    v2, slope1 = activation(first_act)
    v2 = masked(v2)
    for k in range(HK):
        x2[:, k * C1 : (k + 1) * C1] = shifted(v2, k - 2).astype(BF16)
    second_act = dot(x2[...], w2[...])

    v3, slope2 = activation(second_act)
    v3 = masked(v3)
    for k in range(HK):
        x3[:, k * C2 : (k + 1) * C2] = shifted(v3, k - 2).astype(BF16)
    third_act = dot(x3[...], w3[...])

    v4, slope3 = activation(third_act)
    v4 = masked(v4)
    final_taps = [shifted(v4, k - 1)[OWN].astype(BF16) for k in range(PK)]
    wrow = [
        jnp.concatenate([wf[2 * k : 2 * k + 1, :], wf[2 * k + 1 : 2 * k + 2, :]], axis=1) for k in range(PK)
    ]
    total = sum(dot(jnp.broadcast_to(wrow[k], (8, C2)), final_taps[k], 1, 1) for k in range(PK))
    scores[...] = total[0:1]

    low = jnp.where(has_low, hcot[0], 0.0)
    high = jnp.where(has_high, hcot[1], 0.0)
    line = jnp.concatenate([low, cot[...], high], axis=1)
    cots[...] = jnp.zeros_like(cots)
    wfs[...] = jnp.zeros_like(wfs)
    pieces = split3(line)
    for p in range(3):
        for k in range(PK):
            start = FRAMES - HALO - k + 1
            cots[3 * k + p : 3 * k + p + 1, :] = pltpu.roll(pieces[p], 3 * FRAMES - start, 1)[:, : 2 * FRAMES]
            wfs[3 * k + p : 3 * k + p + 1, :] = wrow[k].astype(F32)
        cots[16 + p : 17 + p, 0:FRAMES] = pieces[p][:, FRAMES : 2 * FRAMES]
    upstream = dot(cots[0:16].astype(BF16), wfs[...].astype(BF16), 0, 0)[:ROWS]
    own_cot = cots[16:24, 0:FRAMES].astype(BF16)
    final_grad = [
        jnp.sum(dot(own_cot, final_taps[k]), axis=0, keepdims=True) for k in range(PK)
    ]

    delta = masked(upstream * slope3).astype(BF16)
    grad = dot(x3[OWN], delta[OWN], 0, 0)
    g3s[0], g3s[1] = grad[:, :128], grad[:, 128:]
    for h in range(CORES):
        for r in range(20):
            tst.at[h][pl.ds(r, SHARES, stride=TROWS), :] = g3s.at[h][pl.ds(r, SHARES, stride=20), :]
        for r in range(20, TROWS):
            tst.at[h][pl.ds(r, SHARES, stride=TROWS), :] = jnp.zeros((SHARES, 128), F32)
        for s in range(SHARES):
            a, b, c = s // (NX * NY), (s // NY) % NX, s % NY
            tb[h, b, c, a] = tst[h, s * TROWS : (s + 1) * TROWS].astype(BF16)
    core_t = send(tb.at[1 - core], t0, s0.at[0], q0.at[0], partner)

    def back(delta, weight, width):
        d = delta.astype(F32)
        return sum(
            dot(shifted(d, 2 - k).astype(BF16), weight[k * width : (k + 1) * width], 1, 1)
            for k in range(HK)
        )

    upstream = back(delta, w3, C2)
    delta = masked(upstream * slope2).astype(BF16)
    grad = dot(x2[OWN], delta[OWN], 0, 0)
    g2s[0], g2s[1] = grad[:, :128], grad[:, 128:]
    for h in range(CORES):
        for r in range(10):
            rst.at[h][pl.ds(r, SHARES, stride=RROWS), :] = g2s.at[h][pl.ds(r, SHARES, stride=10), :]

    upstream = back(delta, w2, C1)
    delta = masked(upstream * slope1).astype(BF16)
    for k in range(HK):
        g1s[k * C0 : (k + 1) * C0] = dot(taps1[k][OWN], delta[OWN], 0, 0)
    for r in range(5):
        rst.at[1][pl.ds(10 + r, SHARES, stride=RROWS), :] = g1s[pl.ds(r, SHARES, stride=5), :]

    flat = jnp.concatenate(final_grad, axis=1)
    width = (PK * C2) // SHARES
    offset = lax.broadcasted_iota(jnp.int32, (SHARES, PK * C2), 1) - width * lax.broadcasted_iota(
        jnp.int32, (SHARES, PK * C2), 0
    )
    picked = jnp.where(jnp.logical_and(offset >= 0, offset < width), flat, 0.0).astype(BF16)
    place = lax.broadcasted_iota(jnp.int32, (PK * C2, 128), 0)
    place = place - width * ((place * 5462) >> 16) - lax.broadcasted_iota(jnp.int32, (PK * C2, 128), 1)
    spread = jnp.where(place == 0, 1.0, 0.0).astype(BF16)
    rst.at[1][pl.ds(15, SHARES, stride=RROWS), :] = dot(picked, spread)

    upstream = back(delta, w1, C0)
    delta_squeeze = (upstream[OWN] * squeezed_slope[OWN]).astype(BF16)
    grad = dot(delta_squeeze, hidden, 0, 0)
    for j in range(6):
        rst.at[0][pl.ds(10 + j, SHARES, stride=RROWS), :] = grad[:, j * 128 : (j + 1) * 128]
    for h in range(CORES):
        for s in range(SHARES):
            a, b, c = s // (NX * NY), (s // NY) % NX, s % NY
            rb[h, c, b, a] = rst[h, s * RROWS : (s + 1) * RROWS].astype(BF16)
    core_r = send(rb.at[1 - core], r0, s0.at[1], q0.at[1], partner)

    core_t.wait()
    t1[...] = (tb[core].astype(F32) + t0[...].astype(F32)).astype(BF16)
    along_x = [
        send(t1.at[(px + d) % NX], tx.at[d - 1], sx.at[d - 1], qx.at[d - 1], at(x=(px + d) % NX))
        for d in range(1, NX)
    ]
    core_r.wait()
    r1[...] = (rb[core].astype(F32) + r0[...].astype(F32)).astype(BF16)
    along_y = [
        send(r1.at[(py + d) % NY], ry.at[d - 1], sy.at[d - 1], qy.at[d - 1], at(y=(py + d) % NY))
        for d in range(1, NY)
    ]

    hidden_upstream = dot(delta_squeeze, ws[...])
    projected_grad = normalize_back(hidden_upstream, hidden_normed, hidden_inverse).astype(BF16)
    normed_grad = dot(projected_grad, wp[...], 1, 1)
    fgrad[0] = normalize_back(normed_grad, normed_in, inverse_in)

    for copy in along_x:
        copy.wait()
    acc = t1[px].astype(F32)
    for d in range(NX - 1):
        acc = acc + tx[d].astype(F32)
    t2[...] = acc.astype(BF16)
    along_y2 = [
        send(t2.at[(py + d) % NY], ty.at[d - 1], sy2.at[d - 1], qy2.at[d - 1], at(y=(py + d) % NY))
        for d in range(1, NY)
    ]
    for copy in along_y:
        copy.wait()
    acc = r1[py].astype(F32)
    for d in range(NY - 1):
        acc = acc + ry[d].astype(F32)
    r2[...] = acc.astype(BF16)
    along_x2 = [
        send(r2.at[(px + d) % NX], rx.at[d - 1], sx2.at[d - 1], qx2.at[d - 1], at(x=(px + d) % NX))
        for d in range(1, NX)
    ]
    for copy in along_x2:
        copy.wait()
    acc = r2[px].astype(F32)
    for d in range(NX - 1):
        acc = acc + rx[d].astype(F32)
    zs[:, TROWS:] = acc.astype(BF16)
    for copy in along_y2:
        copy.wait()
    acc = t2[py].astype(F32)
    for d in range(NY - 1):
        acc = acc + ty[d].astype(F32)
    zs[:, :TROWS] = acc.astype(BF16)

    along_z = []
    for d in range(1, NZ):
        target = (pz + d) % NZ
        along_z.append(send(zs.at[target % ZL], zr.at[d], sz.at[d - 1], qz.at[d - 1], at(z=target)))
    for copy in along_z:
        copy.wait()
    zr[0] = zs[zl]
    acc = jnp.zeros((TROWS + RROWS, 128), F32)
    for z in range(NZ):
        acc = acc + zr[(pz + NZ - z) % NZ].astype(F32)
    fin[core] = acc * (1.0 / math.sqrt(FRAMES * SHARES * ZH * CORES))
    send(fin.at[core], fin.at[core], s4, q4, partner).wait()

    fin_out[...] = fin[...]


def finish(scores_in, fgrad_in, fin, scores, fgrad, sq_out, g1_out, g2_out, g3_out, gf_out):
    scores[...] = scores_in[...]
    fgrad[...] = fgrad_in[...]
    g3_out[...] = jnp.concatenate([fin[0, 0:20], fin[1, 0:20]], axis=1)
    g2_out[...] = jnp.concatenate([fin[0, 24:34], fin[1, 24:34]], axis=1)
    g1_out[...] = fin[1, 34:39]
    gf_out[...] = fin[1, 39:40].reshape(128)[: (PK * C2) // SHARES]
    for j in range(6):
        sq_out[:, j * 128 : (j + 1) * 128] = fin[0, 34 + j : 35 + j]


def shards(features, cotangent, wp, ws, w1, w2, w3, wf):
    vmem = pl.BlockSpec(memory_space=pltpu.VMEM)
    operands = (features, cotangent, wp, ws, w1, w2, w3, wf.reshape(6, 128))
    dma = pltpu.SemaphoreType.DMA
    outs = pl.pallas_call(
        kernel,
        out_shape=(
            jax.ShapeDtypeStruct((1, FRAMES), F32),
            jax.ShapeDtypeStruct((1, FRAMES, 512), F32),
            jax.ShapeDtypeStruct((2, TROWS + RROWS, 128), F32),
        ),
        in_specs=[pl.BlockSpec(memory_space=pltpu.HBM)] * 8,
        out_specs=(vmem,) * 3,
        scratch_shapes=[
            pltpu.VMEM((FRAMES, 512), BF16),
            pltpu.VMEM((1, FRAMES), F32),
            pltpu.VMEM((512, 768), BF16),
            pltpu.VMEM((C0, 768), BF16),
            pltpu.VMEM((HK * C0, C1), BF16),
            pltpu.VMEM((HK * C1, C2), BF16),
            pltpu.VMEM((HK * C2, C2), BF16),
            pltpu.VMEM((6, 128), BF16),
            dma((8,)),
            pltpu.VMEM((2, HALO, 512), BF16),
            pltpu.VMEM((2, 1, FRAMES), F32),
            pltpu.VMEM((ROWS, HK * C1), BF16),
            pltpu.VMEM((ROWS, HK * C2), BF16),
            pltpu.VMEM((24, 2 * FRAMES), F32),
            pltpu.VMEM((16, C2), F32),
            pltpu.VMEM((2, HK * C2, 128), F32),
            pltpu.VMEM((2, HK * C1, 128), F32),
            pltpu.VMEM((HK * C0, 128), F32),
            pltpu.VMEM((2, SHARES * TROWS, 128), F32),
            pltpu.VMEM((2, SHARES * RROWS, 128), F32),
            pltpu.VMEM((2, NX, NY, ZL, TROWS, 128), BF16),
            pltpu.VMEM((2, NY, NX, ZL, RROWS, 128), BF16),
            pltpu.VMEM((NX, NY, ZL, TROWS, 128), BF16),
            pltpu.VMEM((NY, NX, ZL, RROWS, 128), BF16),
            pltpu.VMEM((NX, NY, ZL, TROWS, 128), BF16),
            pltpu.VMEM((NY, NX, ZL, RROWS, 128), BF16),
            pltpu.VMEM((NX - 1, NY, ZL, TROWS, 128), BF16),
            pltpu.VMEM((NY - 1, NX, ZL, RROWS, 128), BF16),
            pltpu.VMEM((NY, ZL, TROWS, 128), BF16),
            pltpu.VMEM((NX, ZL, RROWS, 128), BF16),
            pltpu.VMEM((NY - 1, ZL, TROWS, 128), BF16),
            pltpu.VMEM((NX - 1, ZL, RROWS, 128), BF16),
            pltpu.VMEM((ZL, TROWS + RROWS, 128), BF16),
            pltpu.VMEM((NZ, TROWS + RROWS, 128), BF16),
            pltpu.VMEM((2, TROWS + RROWS, 128), F32),
            dma((4,)), dma((4,)),
            dma((2,)), dma((2,)),
            dma((NX - 1,)), dma((NX - 1,)),
            dma((NY - 1,)), dma((NY - 1,)),
            dma((NY - 1,)), dma((NY - 1,)),
            dma((NX - 1,)), dma((NX - 1,)),
            dma((NZ - 1,)), dma((NZ - 1,)),
            dma, dma,
        ],
        compiler_params=pltpu.CompilerParams(collective_id=0, has_side_effects=True, vmem_limit_bytes=24 << 20),
    )(*(pltpu.with_memory_space_constraint(v, pltpu.HBM) for v in operands))
    return pl.pallas_call(
        finish,
        out_shape=(
            jax.ShapeDtypeStruct((1, FRAMES), F32),
            jax.ShapeDtypeStruct((1, FRAMES, 512), F32),
            jax.ShapeDtypeStruct((1, 768), F32),
            jax.ShapeDtypeStruct((5, 128), F32),
            jax.ShapeDtypeStruct((10, 256), F32),
            jax.ShapeDtypeStruct((20, 256), F32),
            jax.ShapeDtypeStruct(((PK * C2) // SHARES,), F32),
        ),
        in_specs=[vmem] * 3,
        out_specs=(vmem,) * 7,
        compiler_params=pltpu.CompilerParams(vmem_limit_bytes=4 << 20),
    )(*outs)


def solution(mesh):
    placed = (P("dp", "seq", None), P("dp", "seq"), P(), P(), P(), P(), P(), P())
    return jax.shard_map(
        shards,
        mesh=mesh,
        in_specs=placed,
        out_specs=(
            P("dp", "seq"),
            P("dp", "seq", None),
            P("seq", None),
            P("seq", None),
            P("seq", None),
            P("seq", None),
            P("seq"),
        ),
        check_vma=False,
    )
```

```python
import math

import jax
import jax.numpy as jnp
from jax import lax
from jax.experimental import pallas as pl
from jax.experimental.pallas import tpu as pltpu
from jax.sharding import PartitionSpec as P

MESH = pl.DeviceIdType.MESH
F32 = jnp.float32
BF16 = jnp.bfloat16

C0, C1, C2 = 64, 128, 256
HK, PK = 5, 3
EPSILON = 1e-05
SLOPE = 0.1
FRAMES = 128
HALO = 16
ROWS = FRAMES + 2 * HALO
OWN = slice(HALO, HALO + FRAMES)

ZH, CORES, ZL, NX, NY = 4, 2, 2, 4, 8
NZ = ZH * ZL
SHARES = ZL * NX * NY
AR, CR, BR = 20, 10, 6


def dot(a, b, ca=1, cb=0):
    return lax.dot_general(a, b, (((ca,), (cb,)), ((), ())), preferred_element_type=F32)


def normalize(values):
    average = jnp.mean(values, axis=-1, keepdims=True)
    centred = values - average
    variance = jnp.mean(centred * centred, axis=-1, keepdims=True)
    inverse = lax.rsqrt(variance + EPSILON)
    return centred * inverse, inverse


def normalize_back(upstream, normed, inverse):
    first_mean = jnp.mean(upstream, axis=-1, keepdims=True)
    second_mean = jnp.mean(upstream * normed, axis=-1, keepdims=True)
    return (upstream - first_mean - normed * second_mean) * inverse


def activation(v):
    cumulative = 0.5 * (1.0 + lax.erf(v * math.sqrt(0.5)))
    density = jnp.exp(-0.5 * v * v) * (1.0 / math.sqrt(2.0 * math.pi))
    value = SLOPE * v + (1.0 - SLOPE) * (v * cumulative)
    slope = SLOPE + (1.0 - SLOPE) * (cumulative + v * density)
    return value, slope


def shifted(v, shift):
    return pltpu.roll(v, (-shift) % v.shape[0], 0) if shift else v


def split3(v):
    hi = v.astype(BF16).astype(F32)
    mid = (v - hi).astype(BF16).astype(F32)
    return hi, mid, (v - hi - mid).astype(BF16).astype(F32)


def kernel(
    feat_in, cot_in, wp_in, ws_in, w1_in, w2_in, w3_in, wf_in,
    scores, fgrad, fin_out,
    feat, cot, wp, ws, w1, w2, w3, wf, in_sem,
    hfeat, hcot, x1, x2, x3, cots, wfs, g3s, g1s, ast, bst,
    ab, a0, a1, ax, a2, ay, cb, c0, c1, cz, c2, cx, cs, c3, cy, bb, b0, b1, by, bs, b2, bx,
    zf, zs, zr, fin,
    hs, hr, s0, q0, sax, qax, say, qay, scz, qcz, scx, qcx, scy, qcy, sby, qby, sbx, qbx, sz, qz, s4, q4, relay,
):
    dp, sq = lax.axis_index("dp"), lax.axis_index("seq")
    zh, core = dp // CORES, dp % CORES
    zl, px, py = sq // (NX * NY), (sq // NY) % NX, sq % NY
    pz = zh * ZL + zl
    count = SHARES

    def at(z=None, x=None, y=None, c=None):
        z = pz if z is None else z
        x = px if x is None else x
        y = py if y is None else y
        c = core if c is None else c
        return ((z // ZL) * CORES + c, (z % ZL) * NX * NY + x * NY + y)

    partner = at(c=1 - core)
    has_low, has_high = sq > 0, sq < count - 1
    before = (jnp.where(has_low, dp, partner[0]), jnp.where(has_low, sq - 1, sq))
    after = (jnp.where(has_high, dp, partner[0]), jnp.where(has_high, sq + 1, sq))
    slot_before, slot_after = jnp.where(has_low, 1, 0), jnp.where(has_high, 0, 1)
    x_up, x_down = at(x=(px + 1) % NX), at(x=(px + NX - 1) % NX)
    y_up, y_down = at(y=(py + 1) % NY), at(y=(py + NY - 1) % NY)
    z_up, z_down = at(z=(pz + 1) % NZ), at(z=(pz + NZ - 1) % NZ)
    peers = [before, after, partner, x_up, x_down, y_up, y_down, z_up, z_down]

    barrier = pltpu.get_barrier_semaphore()
    for peer in peers:
        pl.semaphore_signal(barrier, inc=1, device_id=peer, device_id_type=MESH)
    sources = (feat_in.at[0], cot_in, wp_in, ws_in, w1_in, w2_in, w3_in, wf_in)
    loads = [
        pltpu.make_async_copy(source, target, in_sem.at[i])
        for i, (source, target) in enumerate(zip(sources, (feat, cot, wp, ws, w1, w2, w3, wf)))
    ]
    for load in loads:
        load.start()
    pl.semaphore_wait(barrier, len(peers))

    def send(src, dst, ss, rs, peer):
        copy = pltpu.make_async_remote_copy(
            src_ref=src, dst_ref=dst, send_sem=ss, recv_sem=rs, device_id=peer, device_id_type=MESH
        )
        copy.start()
        return copy

    loads[0].wait()
    loads[1].wait()
    halo = [
        send(feat.at[pl.ds(FRAMES - HALO, HALO)], hfeat.at[slot_after], hs.at[0], hr.at[slot_after], after),
        send(feat.at[pl.ds(0, HALO)], hfeat.at[slot_before], hs.at[1], hr.at[slot_before], before),
        send(cot, hcot.at[slot_after], hs.at[2], hr.at[2 + slot_after], after),
        send(cot, hcot.at[slot_before], hs.at[3], hr.at[2 + slot_before], before),
    ]

    def tell(*signals):
        for i, peer in signals:
            pl.semaphore_signal(relay.at[i], inc=1, device_id=peer, device_id_type=MESH)

    def hear(*indices):
        for i in indices:
            pl.semaphore_wait(relay.at[i], 1)

    tell((0, x_up), (1, y_up), (2, y_down), (3, z_up), (4, z_down))

    def front(rounded):
        projected = dot(rounded, wp[...]).astype(BF16)
        normed, inverse = normalize(projected.astype(F32))
        rounded = normed.astype(BF16)
        return normed, inverse, rounded, dot(rounded, ws[...], 1, 1)

    def chain(v1, masked):
        taps = [shifted(v1, k - 2).astype(BF16) for k in range(HK)] + [jnp.zeros(v1.shape, BF16)]
        t1 = jnp.concatenate(taps, axis=1)
        v2, slope1 = activation(dot(t1[:, : HK * C0], w1[...]))
        v2 = masked(v2)
        t2 = jnp.concatenate([shifted(v2, k - 2).astype(BF16) for k in range(HK)], axis=1)
        v3, slope2 = activation(dot(t2, w2[...]))
        v3 = masked(v3)
        t3 = jnp.concatenate([shifted(v3, k - 2).astype(BF16) for k in range(HK)], axis=1)
        v4, slope3 = activation(dot(t3, w3[...]))
        return (t1, t2, t3), (slope1, slope2, slope3, masked(v4))

    normed_in, inverse_in = normalize(feat[...].astype(F32))
    loads[2].wait()
    loads[3].wait()
    hidden_normed, hidden_inverse, hidden, squeezed = front(normed_in.astype(BF16))
    v1, squeezed_slope = activation(squeezed)
    for i in (4, 5, 6, 7):
        loads[i].wait()
    own_taps, own_rows = chain(v1, lambda v: v)
    for target, value in zip((x1, x2, x3), own_taps):
        target[...] = value
    for copy in halo:
        copy.wait_send()
    for i in range(2):
        for source, target, sem in ((feat.at[pl.ds(0, HALO)], hfeat.at[i], i), (cot, hcot.at[i], 2 + i)):
            pltpu.make_async_remote_copy(
                src_ref=source,
                dst_ref=target,
                send_sem=hs.at[sem],
                recv_sem=hr.at[sem],
                device_id=after,
                device_id_type=MESH,
            ).wait_recv()
    hear(0, 1, 2, 3, 4)
    tell((5, y_up), (6, y_down), (7, z_up), (8, z_down))
    edge = jnp.concatenate(
        [
            jnp.where(has_low, hfeat[0].astype(F32), 0.0),
            jnp.where(has_high, hfeat[1].astype(F32), 0.0),
        ],
        axis=0,
    )
    edge = activation(front(normalize(edge)[0].astype(BF16))[3])[0]
    edge = jnp.concatenate([edge[:HALO], v1[:HALO], v1[FRAMES - HALO :], edge[HALO:]], axis=0)
    row = lax.broadcasted_iota(jnp.int32, (4 * HALO, 1), 0)
    inside = jnp.logical_and(row >= jnp.where(has_low, 0, HALO), row < jnp.where(has_high, 4 * HALO, 3 * HALO))
    edge_taps, edge_rows = chain(edge, lambda v: jnp.where(inside, v, 0.0))
    for target, value in zip((x1, x2, x3), edge_taps):
        target[0:8] = value[HALO : HALO + 8]
        target[FRAMES - 8 : FRAMES] = value[3 * HALO - 8 : 3 * HALO]
    slope1, slope2, slope3, v4 = (
        jnp.concatenate([strip[: HALO + 8], mid[8 : FRAMES - 8], strip[3 * HALO - 8 :]], axis=0)
        for strip, mid in zip(edge_rows, own_rows)
    )
    row = lax.broadcasted_iota(jnp.int32, (ROWS, 1), 0)
    first_row = jnp.where(has_low, 0, HALO)
    last_row = jnp.where(has_high, ROWS, HALO + FRAMES)
    inside_all = jnp.logical_and(row >= first_row, row < last_row)

    def masked(v):
        return jnp.where(inside_all, v, 0.0)

    final_taps = [shifted(v4, k - 1)[OWN].astype(BF16) for k in range(PK)]
    wrow = [
        jnp.concatenate([wf[2 * k : 2 * k + 1, :], wf[2 * k + 1 : 2 * k + 2, :]], axis=1) for k in range(PK)
    ]
    total = sum(dot(jnp.broadcast_to(wrow[k], (8, C2)), final_taps[k], 1, 1) for k in range(PK))
    scores[...] = total[0:1]

    low = jnp.where(has_low, hcot[0], 0.0)
    high = jnp.where(has_high, hcot[1], 0.0)
    line = jnp.concatenate([low, cot[...], high], axis=1)
    cots[...] = jnp.zeros_like(cots)
    wfs[...] = jnp.zeros_like(wfs)
    pieces = split3(line)
    for p in range(3):
        for k in range(PK):
            start = FRAMES - HALO - k + 1
            cots[3 * k + p : 3 * k + p + 1, :] = pltpu.roll(pieces[p], 3 * FRAMES - start, 1)[:, : 2 * FRAMES]
            wfs[3 * k + p : 3 * k + p + 1, :] = wrow[k].astype(F32)
        cots[16 + p : 17 + p, 0:FRAMES] = pieces[p][:, FRAMES : 2 * FRAMES]
    upstream = dot(cots[0:16].astype(BF16), wfs[...].astype(BF16), 0, 0)[:ROWS]
    own_cot = cots[16:24, 0:FRAMES].astype(BF16)
    final_grad = [
        jnp.sum(dot(own_cot, final_taps[k]), axis=0, keepdims=True) for k in range(PK)
    ]

    hear(5, 6, 7, 8)
    tell((9, y_up), (10, z_up))
    delta = masked(upstream * slope3).astype(BF16)
    grad = dot(x3[...], delta[OWN], 0, 0)
    g3s[0], g3s[1] = grad[:, :128], grad[:, 128:]
    plane = NX * NY
    for h in range(CORES):
        for a in range(ZL):
            for r in range(AR):
                ast.at[h][pl.ds(a * AR + r, plane, stride=ZL * AR), :] = g3s.at[h][
                    pl.ds(a * plane * AR + r, plane, stride=AR), :
                ]
        for x in range(NX):
            ab[h, x] = ast[h, x * NY * ZL * AR : (x + 1) * NY * ZL * AR].astype(BF16)
    core_a = send(ab.at[1 - core], a0, s0.at[0], q0.at[0], partner)

    def back(delta, weight, width):
        d = delta.astype(F32)
        return sum(
            dot(shifted(d, 2 - k).astype(BF16), weight[k * width : (k + 1) * width], 1, 1)
            for k in range(HK)
        )

    def back_narrow(delta, weight, width):
        wide = dot(delta, weight[...], 1, 1)
        return sum(shifted(wide[:, k * width : (k + 1) * width], 2 - k) for k in range(HK))

    upstream = back(delta, w3, C2)
    delta = masked(upstream * slope2).astype(BF16)
    grad = dot(x2[...], delta[OWN], 0, 0)
    for h in range(CORES):
        cb[h] = grad[:, h * 128 : (h + 1) * 128].astype(BF16).reshape(ZL, NX, NY * CR, 128)
    core_c = send(cb.at[1 - core], c0, s0.at[1], q0.at[1], partner)

    upstream = back_narrow(delta, w2, C1)
    delta = masked(upstream * slope1).astype(BF16)
    g1s[...] = dot(x1[...], delta[OWN], 0, 0)
    lines = [(a * plane + x * NY, (x * ZL + a) * BR) for a in range(ZL) for x in range(NX)]
    step = NX * ZL * BR
    for share, row in lines:
        for r in range(5):
            bst.at[1][pl.ds(row + r, NY, stride=step), :] = g1s[pl.ds(5 * share + r, NY, stride=5), :]

    flat = jnp.concatenate(final_grad, axis=1)
    width = (PK * C2) // SHARES
    offset = lax.broadcasted_iota(jnp.int32, (SHARES, PK * C2), 1) - width * lax.broadcasted_iota(
        jnp.int32, (SHARES, PK * C2), 0
    )
    picked = jnp.where(jnp.logical_and(offset >= 0, offset < width), flat, 0.0).astype(BF16)
    place = lax.broadcasted_iota(jnp.int32, (PK * C2, 128), 0)
    place = place - width * ((place * 5462) >> 16) - lax.broadcasted_iota(jnp.int32, (PK * C2, 128), 1)
    spread = jnp.where(place == 0, 1.0, 0.0).astype(BF16)
    spread = dot(picked, spread)
    for share, row in lines:
        bst.at[1][pl.ds(row + 5, NY, stride=step), :] = spread[share : share + NY]

    upstream = back_narrow(delta, w1, C0)
    delta_squeeze = (upstream[OWN] * squeezed_slope).astype(BF16)
    grad = dot(delta_squeeze, hidden, 0, 0)
    for share, row in lines:
        for j in range(BR):
            bst.at[0][pl.ds(row + j, NY, stride=step), :] = grad[share : share + NY, j * 128 : (j + 1) * 128]
    for h in range(CORES):
        for y in range(NY):
            bb[h, y] = bst[h, y * step : (y + 1) * step].astype(BF16)
    core_b = send(bb.at[1 - core], b0, s0.at[2], q0.at[2], partner)

    def along_x(source, target, ss, rs):
        return [
            send(source.at[(px + d) % NX], target.at[d - 1], ss.at[d - 1], rs.at[d - 1], at(x=(px + d) % NX))
            for d in range(1, NX)
        ]

    def along_y(source, target, ss, rs):
        return [
            send(source.at[(py + d) % NY], target.at[d - 1], ss.at[d - 1], rs.at[d - 1], at(y=(py + d) % NY))
            for d in range(1, NY)
        ]

    def gathered(copies, own, arrived):
        for copy in copies:
            copy.wait()
        acc = own.astype(F32)
        for d in range(len(copies)):
            acc = acc + arrived[d].astype(F32)
        return acc

    hear(9, 10)
    core_a.wait()
    a1[...] = (ab[core].astype(F32) + a0[...].astype(F32)).astype(BF16)
    a_x = along_x(a1, ax, sax, qax)
    core_c.wait()
    c1[...] = (cb[core].astype(F32) + c0[...].astype(F32)).astype(BF16)
    pair = pz + 1 - 2 * zl
    c_z = send(c1.at[1 - zl], cz, scz, qcz, at(z=pair))
    core_b.wait()
    b1[...] = (bb[core].astype(F32) + b0[...].astype(F32)).astype(BF16)
    b_y = along_y(b1, by, sby, qby)

    hidden_upstream = dot(delta_squeeze, ws[...])
    projected_grad = normalize_back(hidden_upstream, hidden_normed, hidden_inverse).astype(BF16)
    normed_grad = dot(projected_grad, wp[...], 1, 1)
    fgrad[0] = normalize_back(normed_grad, normed_in, inverse_in)

    c_z.wait()
    c2[...] = (c1[zl].astype(F32) + cz[...].astype(F32)).astype(BF16)
    c_x = along_x(c2, cx, scx, qcx)
    a2[...] = gathered(a_x, a1[px], ax).astype(BF16).reshape(NY, ZL * AR, 128)
    a_y = along_y(a2, ay, say, qay)
    bs[0:step] = gathered(b_y, b1[py], by)
    bs[step:] = jnp.zeros((8, 128), F32)
    for x in range(NX):
        b2[x] = bs[x * ZL * BR : x * ZL * BR + 16].astype(BF16)
    b_x = along_x(b2, bx, sbx, qbx)
    cs[0 : NY * CR] = gathered(c_x, c2[px], cx)
    cs[NY * CR :] = jnp.zeros((8, 128), F32)
    for y in range(NY):
        c3[y] = cs[y * CR : y * CR + 16].astype(BF16)
    c_y = along_y(c3, cy, scy, qcy)

    zf[...] = jnp.zeros_like(zf)
    total = gathered(b_x, b2[px], bx)
    for a in range(ZL):
        zf[a, AR : AR + BR] = total[a * BR : (a + 1) * BR]
    total = gathered(a_y, a2[py], ay)
    for a in range(ZL):
        zf[a, 0:AR] = total[a * AR : (a + 1) * AR]
    total = gathered(c_y, c3[py], cy)
    for a in range(ZL):
        zf[a, 32:48] = total
    zs[...] = zf[...].astype(BF16)

    along_z = []
    for d in range(1, NZ):
        target = (pz + d) % NZ
        rows = 32 if d % ZL else 48
        along_z.append(
            send(
                zs.at[target % ZL, pl.ds(0, rows)], zr.at[d, pl.ds(0, rows)], sz.at[d - 1], qz.at[d - 1], at(z=target)
            )
        )
    for copy in along_z:
        copy.wait()
    zr[0] = zs[zl]
    scale = 1.0 / math.sqrt(FRAMES * SHARES * ZH * CORES)
    acc = jnp.zeros((32, 128), F32)
    for z in range(NZ):
        acc = acc + zr[(pz + NZ - z) % NZ, 0:32].astype(F32)
    fin[core, 0:32] = acc * scale
    acc = jnp.zeros((16, 128), F32)
    for z in range(ZH):
        acc = acc + zr[(pz + NZ - (z * ZL + zl)) % NZ, 32:48].astype(F32)
    fin[core, 32:48] = acc * scale
    send(fin.at[core], fin.at[core], s4, q4, partner).wait()

    fin_out[...] = fin[...]


def finish(scores_in, fgrad_in, fin, scores, fgrad, sq_out, g1_out, g2_out, g3_out, gf_out):
    scores[...] = scores_in[...]
    fgrad[...] = fgrad_in[...]
    g3_out[...] = jnp.concatenate([fin[0, 0:20], fin[1, 0:20]], axis=1)
    g2_out[...] = jnp.concatenate([fin[0, 32:42], fin[1, 32:42]], axis=1)
    g1_out[...] = fin[1, 20:25]
    gf_out[...] = fin[1, 25:26].reshape(128)[: (PK * C2) // SHARES]
    for j in range(6):
        sq_out[:, j * 128 : (j + 1) * 128] = fin[0, 20 + j : 21 + j]


def shards(features, cotangent, wp, ws, w1, w2, w3, wf):
    vmem = pl.BlockSpec(memory_space=pltpu.VMEM)
    operands = (features, cotangent, wp, ws, w1, w2, w3, wf.reshape(6, 128))
    dma = pltpu.SemaphoreType.DMA
    outs = pl.pallas_call(
        kernel,
        out_shape=(
            jax.ShapeDtypeStruct((1, FRAMES), F32),
            jax.ShapeDtypeStruct((1, FRAMES, 512), F32),
            jax.ShapeDtypeStruct((2, 48, 128), F32),
        ),
        in_specs=[pl.BlockSpec(memory_space=pltpu.HBM)] * 8,
        out_specs=(vmem,) * 3,
        scratch_shapes=[
            pltpu.VMEM((FRAMES, 512), BF16),
            pltpu.VMEM((1, FRAMES), F32),
            pltpu.VMEM((512, 768), BF16),
            pltpu.VMEM((C0, 768), BF16),
            pltpu.VMEM((HK * C0, C1), BF16),
            pltpu.VMEM((HK * C1, C2), BF16),
            pltpu.VMEM((HK * C2, C2), BF16),
            pltpu.VMEM((6, 128), BF16),
            dma((8,)),
            pltpu.VMEM((2, HALO, 512), BF16),
            pltpu.VMEM((2, 1, FRAMES), F32),
            pltpu.VMEM((FRAMES, (HK + 1) * C0), BF16),
            pltpu.VMEM((FRAMES, HK * C1), BF16),
            pltpu.VMEM((FRAMES, HK * C2), BF16),
            pltpu.VMEM((24, 2 * FRAMES), F32),
            pltpu.VMEM((16, C2), F32),
            pltpu.VMEM((2, HK * C2, 128), F32),
            pltpu.VMEM(((HK + 1) * C0, 128), F32),
            pltpu.VMEM((2, SHARES * AR, 128), F32),
            pltpu.VMEM((2, SHARES * BR, 128), F32),
            pltpu.VMEM((2, NX, NY * ZL * AR, 128), BF16),
            pltpu.VMEM((NX, NY * ZL * AR, 128), BF16),
            pltpu.VMEM((NX, NY * ZL * AR, 128), BF16),
            pltpu.VMEM((NX - 1, NY * ZL * AR, 128), BF16),
            pltpu.VMEM((NY, ZL * AR, 128), BF16),
            pltpu.VMEM((NY - 1, ZL * AR, 128), BF16),
            pltpu.VMEM((2, ZL, NX, NY * CR, 128), BF16),
            pltpu.VMEM((ZL, NX, NY * CR, 128), BF16),
            pltpu.VMEM((ZL, NX, NY * CR, 128), BF16),
            pltpu.VMEM((NX, NY * CR, 128), BF16),
            pltpu.VMEM((NX, NY * CR, 128), BF16),
            pltpu.VMEM((NX - 1, NY * CR, 128), BF16),
            pltpu.VMEM((NY * CR + 8, 128), F32),
            pltpu.VMEM((NY, 16, 128), BF16),
            pltpu.VMEM((NY - 1, 16, 128), BF16),
            pltpu.VMEM((2, NY, NX * ZL * BR, 128), BF16),
            pltpu.VMEM((NY, NX * ZL * BR, 128), BF16),
            pltpu.VMEM((NY, NX * ZL * BR, 128), BF16),
            pltpu.VMEM((NY - 1, NX * ZL * BR, 128), BF16),
            pltpu.VMEM((NX * ZL * BR + 8, 128), F32),
            pltpu.VMEM((NX, 16, 128), BF16),
            pltpu.VMEM((NX - 1, 16, 128), BF16),
            pltpu.VMEM((ZL, 48, 128), F32),
            pltpu.VMEM((ZL, 48, 128), BF16),
            pltpu.VMEM((NZ, 48, 128), BF16),
            pltpu.VMEM((2, 48, 128), F32),
            dma((4,)), dma((4,)),
            dma((3,)), dma((3,)),
            dma((NX - 1,)), dma((NX - 1,)),
            dma((NY - 1,)), dma((NY - 1,)),
            dma, dma,
            dma((NX - 1,)), dma((NX - 1,)),
            dma((NY - 1,)), dma((NY - 1,)),
            dma((NY - 1,)), dma((NY - 1,)),
            dma((NX - 1,)), dma((NX - 1,)),
            dma((NZ - 1,)), dma((NZ - 1,)),
            dma, dma,
            pltpu.SemaphoreType.REGULAR((11,)),
        ],
        compiler_params=pltpu.CompilerParams(collective_id=0, has_side_effects=True, vmem_limit_bytes=24 << 20),
    )(*(pltpu.with_memory_space_constraint(v, pltpu.HBM) for v in operands))
    return pl.pallas_call(
        finish,
        out_shape=(
            jax.ShapeDtypeStruct((1, FRAMES), F32),
            jax.ShapeDtypeStruct((1, FRAMES, 512), F32),
            jax.ShapeDtypeStruct((1, 768), F32),
            jax.ShapeDtypeStruct((5, 128), F32),
            jax.ShapeDtypeStruct((10, 256), F32),
            jax.ShapeDtypeStruct((20, 256), F32),
            jax.ShapeDtypeStruct(((PK * C2) // SHARES,), F32),
        ),
        in_specs=[vmem] * 3,
        out_specs=(vmem,) * 7,
        compiler_params=pltpu.CompilerParams(vmem_limit_bytes=4 << 20),
    )(*outs)


def solution(mesh):
    placed = (P("dp", "seq", None), P("dp", "seq"), P(), P(), P(), P(), P(), P())
    return jax.shard_map(
        shards,
        mesh=mesh,
        in_specs=placed,
        out_specs=(
            P("dp", "seq"),
            P("dp", "seq", None),
            P("seq", None),
            P("seq", None),
            P("seq", None),
            P("seq", None),
            P("seq"),
        ),
        check_vma=False,
    )
```

```python
import math

import jax
import jax.numpy as jnp
from jax import lax
from jax.experimental import pallas as pl
from jax.experimental.pallas import tpu as pltpu
from jax.sharding import PartitionSpec as P

MESH = pl.DeviceIdType.MESH
F32 = jnp.float32
BF16 = jnp.bfloat16

C0, C1, C2 = 64, 128, 256
HK, PK = 5, 3
EPSILON = 1e-05
SLOPE = 0.1
FRAMES = 128
HALO = 16
ROWS = FRAMES + 2 * HALO
OWN = slice(HALO, HALO + FRAMES)

ZH, CORES, ZL, NX, NY = 4, 2, 2, 4, 8
NZ = ZH * ZL
SHARES = ZL * NX * NY
AR, CR, BR = 20, 8, 8
SECOND = 10


def dot(a, b, ca=1, cb=0):
    return lax.dot_general(a, b, (((ca,), (cb,)), ((), ())), preferred_element_type=F32)


def normalize(values):
    average = jnp.mean(values, axis=-1, keepdims=True)
    centred = values - average
    variance = jnp.mean(centred * centred, axis=-1, keepdims=True)
    inverse = lax.rsqrt(variance + EPSILON)
    return centred * inverse, inverse


def normalize_back(upstream, normed, inverse):
    first_mean = jnp.mean(upstream, axis=-1, keepdims=True)
    second_mean = jnp.mean(upstream * normed, axis=-1, keepdims=True)
    return (upstream - first_mean - normed * second_mean) * inverse


def activation(v):
    cumulative = 0.5 * (1.0 + lax.erf(v * math.sqrt(0.5)))
    density = jnp.exp(-0.5 * v * v) * (1.0 / math.sqrt(2.0 * math.pi))
    value = SLOPE * v + (1.0 - SLOPE) * (v * cumulative)
    slope = SLOPE + (1.0 - SLOPE) * (cumulative + v * density)
    return value, slope


def shifted(v, shift):
    return pltpu.roll(v, (-shift) % v.shape[0], 0) if shift else v


def split3(v):
    hi = v.astype(BF16).astype(F32)
    mid = (v - hi).astype(BF16).astype(F32)
    return hi, mid, (v - hi - mid).astype(BF16).astype(F32)


def kernel(
    feat_in, cot_in, wp_in, ws_in, w1_in, w2_in, w3_in, wf_in,
    scores, fgrad, fin_out,
    feat, cot, wp, ws, w1, w2, w3, wf, in_sem,
    hfeat, hcot, x1, x2, x3, cots, wfs, g3s, g2s, g1s, ast, cst, bst,
    ab, a0, a1, ax, a2, ay, cb, c0, c1, cz, c2, cx, c3, cy, bb, b0, b1, by, b2, bx,
    zf, zs, zr, zc, fin,
    hs, hr, s0, q0, sax, qax, say, qay, scz, qcz, scx, qcx, scy, qcy, sby, qby, sbx, qbx, sz, qz, szc, qzc, s4, q4, relay,
):
    dp, sq = lax.axis_index("dp"), lax.axis_index("seq")
    zh, core = dp // CORES, dp % CORES
    zl, px, py = sq // (NX * NY), (sq // NY) % NX, sq % NY
    pz = zh * ZL + zl
    count = SHARES

    def at(z=None, x=None, y=None, c=None):
        z = pz if z is None else z
        x = px if x is None else x
        y = py if y is None else y
        c = core if c is None else c
        return ((z // ZL) * CORES + c, (z % ZL) * NX * NY + x * NY + y)

    partner = at(c=1 - core)
    has_low, has_high = sq > 0, sq < count - 1
    before = (jnp.where(has_low, dp, partner[0]), jnp.where(has_low, sq - 1, sq))
    after = (jnp.where(has_high, dp, partner[0]), jnp.where(has_high, sq + 1, sq))
    slot_before, slot_after = jnp.where(has_low, 1, 0), jnp.where(has_high, 0, 1)
    x_up, x_down = at(x=(px + 1) % NX), at(x=(px + NX - 1) % NX)
    y_up, y_down = at(y=(py + 1) % NY), at(y=(py + NY - 1) % NY)
    z_up, z_down = at(z=(pz + 1) % NZ), at(z=(pz + NZ - 1) % NZ)
    peers = [before, after, partner, x_up, x_down, y_up, y_down, z_up, z_down]

    barrier = pltpu.get_barrier_semaphore()
    for peer in peers:
        pl.semaphore_signal(barrier, inc=1, device_id=peer, device_id_type=MESH)
    sources = (feat_in.at[0], cot_in, wp_in, ws_in, w1_in, w2_in, w3_in, wf_in)
    loads = [
        pltpu.make_async_copy(source, target, in_sem.at[i])
        for i, (source, target) in enumerate(zip(sources, (feat, cot, wp, ws, w1, w2, w3, wf)))
    ]
    for load in loads:
        load.start()
    pl.semaphore_wait(barrier, len(peers))

    def send(src, dst, ss, rs, peer):
        copy = pltpu.make_async_remote_copy(
            src_ref=src, dst_ref=dst, send_sem=ss, recv_sem=rs, device_id=peer, device_id_type=MESH
        )
        copy.start()
        sent.append(copy)
        return copy

    sent = []

    loads[0].wait()
    loads[1].wait()
    halo = [
        send(feat.at[pl.ds(FRAMES - HALO, HALO)], hfeat.at[slot_after], hs.at[0], hr.at[slot_after], after),
        send(feat.at[pl.ds(0, HALO)], hfeat.at[slot_before], hs.at[1], hr.at[slot_before], before),
        send(cot, hcot.at[slot_after], hs.at[2], hr.at[2 + slot_after], after),
        send(cot, hcot.at[slot_before], hs.at[3], hr.at[2 + slot_before], before),
    ]

    def tell(*signals):
        for i, peer in signals:
            pl.semaphore_signal(relay.at[i], inc=1, device_id=peer, device_id_type=MESH)

    def hear(*indices):
        for i in indices:
            pl.semaphore_wait(relay.at[i], 1)

    tell((0, x_up), (1, y_up), (2, y_down), (3, z_up), (4, z_down))

    def front(rounded):
        projected = dot(rounded, wp[...]).astype(BF16)
        normed, inverse = normalize(projected.astype(F32))
        rounded = normed.astype(BF16)
        return normed, inverse, rounded, dot(rounded, ws[...], 1, 1)

    def chain(v1, masked):
        taps = [shifted(v1, k - 2).astype(BF16) for k in range(HK)] + [jnp.zeros(v1.shape, BF16)]
        t1 = jnp.concatenate(taps, axis=1)
        v2, slope1 = activation(dot(t1[:, : HK * C0], w1[...]))
        v2 = masked(v2)
        t2 = jnp.concatenate([shifted(v2, k - 2).astype(BF16) for k in range(HK)], axis=1)
        v3, slope2 = activation(dot(t2, w2[...]))
        v3 = masked(v3)
        t3 = jnp.concatenate([shifted(v3, k - 2).astype(BF16) for k in range(HK)], axis=1)
        v4, slope3 = activation(dot(t3, w3[...]))
        return (t1, t2, t3), (slope1, slope2, slope3, masked(v4))

    normed_in, inverse_in = normalize(feat[...].astype(F32))
    loads[2].wait()
    loads[3].wait()
    hidden_normed, hidden_inverse, hidden, squeezed = front(normed_in.astype(BF16))
    v1, squeezed_slope = activation(squeezed)
    for i in (4, 5, 6, 7):
        loads[i].wait()
    own_taps, own_rows = chain(v1, lambda v: v)
    for target, value in zip((x1, x2, x3), own_taps):
        target[...] = value
    for i in range(2):
        for source, target, sem in ((feat.at[pl.ds(0, HALO)], hfeat.at[i], i), (cot, hcot.at[i], 2 + i)):
            pltpu.make_async_remote_copy(
                src_ref=source,
                dst_ref=target,
                send_sem=hs.at[sem],
                recv_sem=hr.at[sem],
                device_id=after,
                device_id_type=MESH,
            ).wait_recv()
    hear(0, 1, 2, 3, 4)
    tell((5, y_up), (6, y_down), (7, z_up), (8, z_down))
    edge = jnp.concatenate(
        [
            jnp.where(has_low, hfeat[0].astype(F32), 0.0),
            jnp.where(has_high, hfeat[1].astype(F32), 0.0),
        ],
        axis=0,
    )
    edge = activation(front(normalize(edge)[0].astype(BF16))[3])[0]
    edge = jnp.concatenate([edge[:HALO], v1[:HALO], v1[FRAMES - HALO :], edge[HALO:]], axis=0)
    row = lax.broadcasted_iota(jnp.int32, (4 * HALO, 1), 0)
    inside = jnp.logical_and(row >= jnp.where(has_low, 0, HALO), row < jnp.where(has_high, 4 * HALO, 3 * HALO))
    edge_taps, edge_rows = chain(edge, lambda v: jnp.where(inside, v, 0.0))
    for target, value in zip((x1, x2, x3), edge_taps):
        target[0:8] = value[HALO : HALO + 8]
        target[FRAMES - 8 : FRAMES] = value[3 * HALO - 8 : 3 * HALO]
    slope1, slope2, slope3, v4 = (
        jnp.concatenate([strip[: HALO + 8], mid[8 : FRAMES - 8], strip[3 * HALO - 8 :]], axis=0)
        for strip, mid in zip(edge_rows, own_rows)
    )
    row = lax.broadcasted_iota(jnp.int32, (ROWS, 1), 0)
    first_row = jnp.where(has_low, 0, HALO)
    last_row = jnp.where(has_high, ROWS, HALO + FRAMES)
    inside_all = jnp.logical_and(row >= first_row, row < last_row)

    def masked(v):
        return jnp.where(inside_all, v, 0.0)

    wrow = [
        jnp.concatenate([wf[2 * k : 2 * k + 1, :], wf[2 * k + 1 : 2 * k + 2, :]], axis=1) for k in range(PK)
    ]
    low = jnp.where(has_low, hcot[0], 0.0)
    high = jnp.where(has_high, hcot[1], 0.0)
    line = jnp.concatenate([low, cot[...], high], axis=1)
    cots[...] = jnp.zeros_like(cots)
    wfs[...] = jnp.zeros_like(wfs)
    pieces = split3(line)
    for p in range(3):
        for k in range(PK):
            start = FRAMES - HALO - k + 1
            cots[3 * k + p : 3 * k + p + 1, :] = pltpu.roll(pieces[p], 3 * FRAMES - start, 1)[:, : 2 * FRAMES]
            wfs[3 * k + p : 3 * k + p + 1, :] = wrow[k].astype(F32)
        cots[16 + p : 17 + p, 0:FRAMES] = pieces[p][:, FRAMES : 2 * FRAMES]
    upstream = dot(cots[0:16].astype(BF16), wfs[...].astype(BF16), 0, 0)[:ROWS]
    hear(5, 6, 7, 8)
    tell((9, y_up), (10, z_up))
    delta = masked(upstream * slope3).astype(BF16)
    grad = dot(x3[...], delta[OWN], 0, 0)
    g3s[0], g3s[1] = grad[:, :128], grad[:, 128:]
    plane = NX * NY
    for h in range(CORES):
        for a in range(ZL):
            for r in range(AR):
                ast.at[h][pl.ds(a * AR + r, plane, stride=ZL * AR), :] = g3s.at[h][
                    pl.ds(a * plane * AR + r, plane, stride=AR), :
                ]
        for x in range(NX):
            ab[h, x] = ast[h, x * NY * ZL * AR : (x + 1) * NY * ZL * AR].astype(BF16)
    core_a = send(ab.at[1 - core], a0, s0.at[0], q0.at[0], partner)

    def back(delta, weight, width):
        d = delta.astype(F32)
        return sum(
            dot(shifted(d, 2 - k).astype(BF16), weight[k * width : (k + 1) * width], 1, 1)
            for k in range(HK)
        )

    def back_narrow(delta, weight, width):
        wide = dot(delta, weight[...], 1, 1)
        return sum(shifted(wide[:, k * width : (k + 1) * width], 2 - k) for k in range(HK))

    upstream = back(delta, w3, C2)
    delta = masked(upstream * slope2).astype(BF16)
    grad = dot(x2[...], delta[OWN], 0, 0)
    for h in range(CORES):
        g2s[h] = grad[:, h * 128 : (h + 1) * 128]
        for r in range(CR):
            cst.at[h][pl.ds(r, SHARES, stride=CR), :] = g2s.at[h][pl.ds(r, SHARES, stride=SECOND), :]
        cb[h] = cst[h].astype(BF16).reshape(ZL, NX, NY * CR, 128)
    core_c = send(cb.at[1 - core], c0, s0.at[1], q0.at[1], partner)

    final_taps = [shifted(v4, k - 1)[OWN].astype(BF16) for k in range(PK)]
    total = sum(dot(jnp.broadcast_to(wrow[k], (8, C2)), final_taps[k], 1, 1) for k in range(PK))
    scores[...] = total[0:1]


    own_cot = cots[16:24, 0:FRAMES].astype(BF16)
    final_grad = [
        jnp.sum(dot(own_cot, final_taps[k]), axis=0, keepdims=True) for k in range(PK)
    ]

    upstream = back_narrow(delta, w2, C1)
    delta = masked(upstream * slope1).astype(BF16)
    g1s[...] = dot(x1[...], delta[OWN], 0, 0)
    lines = [(a * plane + x * NY, (x * ZL + a) * BR) for a in range(ZL) for x in range(NX)]
    step = NX * ZL * BR
    for h in range(CORES):
        for share, row in lines:
            for r in range(CR, SECOND):
                bst.at[h][pl.ds(row + r - 2, NY, stride=step), :] = g2s.at[h][
                    pl.ds(SECOND * share + r, NY, stride=SECOND), :
                ]
    for share, row in lines:
        for r in range(5):
            bst.at[1][pl.ds(row + r, NY, stride=step), :] = g1s[pl.ds(5 * share + r, NY, stride=5), :]

    flat = jnp.concatenate(final_grad, axis=1)
    width = (PK * C2) // SHARES
    offset = lax.broadcasted_iota(jnp.int32, (SHARES, PK * C2), 1) - width * lax.broadcasted_iota(
        jnp.int32, (SHARES, PK * C2), 0
    )
    picked = jnp.where(jnp.logical_and(offset >= 0, offset < width), flat, 0.0).astype(BF16)
    place = lax.broadcasted_iota(jnp.int32, (PK * C2, 128), 0)
    place = place - width * ((place * 5462) >> 16) - lax.broadcasted_iota(jnp.int32, (PK * C2, 128), 1)
    spread = jnp.where(place == 0, 1.0, 0.0).astype(BF16)
    spread = dot(picked, spread)
    for share, row in lines:
        bst.at[1][pl.ds(row + 5, NY, stride=step), :] = spread[share : share + NY]

    upstream = back_narrow(delta, w1, C0)
    delta_squeeze = (upstream[OWN] * squeezed_slope).astype(BF16)
    grad = dot(delta_squeeze, hidden, 0, 0)
    for share, row in lines:
        for j in range(6):
            bst.at[0][pl.ds(row + j, NY, stride=step), :] = grad[share : share + NY, j * 128 : (j + 1) * 128]
    for h in range(CORES):
        for y in range(NY):
            bb[h, y] = bst[h, y * step : (y + 1) * step].astype(BF16)
    core_b = send(bb.at[1 - core], b0, s0.at[2], q0.at[2], partner)

    def along_x(source, target, ss, rs):
        return [
            send(source.at[(px + d) % NX], target.at[d - 1], ss.at[d - 1], rs.at[d - 1], at(x=(px + d) % NX))
            for d in range(1, NX)
        ]

    def along_y(source, target, ss, rs):
        return [
            send(source.at[(py + d) % NY], target.at[d - 1], ss.at[d - 1], rs.at[d - 1], at(y=(py + d) % NY))
            for d in range(1, NY)
        ]

    def gathered(copies, own, arrived):
        for copy in copies:
            copy.wait_recv()
        acc = own.astype(F32)
        for d in range(len(copies)):
            acc = acc + arrived[d].astype(F32)
        return acc

    hear(9, 10)
    core_a.wait_recv()
    a1[...] = (ab[core].astype(F32) + a0[...].astype(F32)).astype(BF16)
    a_x = along_x(a1, ax, sax, qax)
    core_c.wait_recv()
    c1[...] = (cb[core].astype(F32) + c0[...].astype(F32)).astype(BF16)
    pair = pz + 1 - 2 * zl
    c_z = send(c1.at[1 - zl], cz, scz, qcz, at(z=pair))
    core_b.wait_recv()
    b1[...] = (bb[core].astype(F32) + b0[...].astype(F32)).astype(BF16)
    b_y = along_y(b1, by, sby, qby)

    hidden_upstream = dot(delta_squeeze, ws[...])
    projected_grad = normalize_back(hidden_upstream, hidden_normed, hidden_inverse).astype(BF16)
    normed_grad = dot(projected_grad, wp[...], 1, 1)
    fgrad[0] = normalize_back(normed_grad, normed_in, inverse_in)

    c_z.wait_recv()
    c2[...] = (c1[zl].astype(F32) + cz[...].astype(F32)).astype(BF16)
    c_x = along_x(c2, cx, scx, qcx)
    a2[...] = gathered(a_x, a1[px], ax).astype(BF16).reshape(NY, ZL * AR, 128)
    a_y = along_y(a2, ay, say, qay)
    b2[...] = gathered(b_y, b1[py], by).astype(BF16).reshape(NX, ZL * BR, 128)
    b_x = along_x(b2, bx, sbx, qbx)
    c3[...] = gathered(c_x, c2[px], cx).astype(BF16).reshape(NY, CR, 128)
    c_y = along_y(c3, cy, scy, qcy)

    zf[...] = jnp.zeros_like(zf)
    total = gathered(b_x, b2[px], bx)
    for a in range(ZL):
        zf[a, AR : AR + BR] = total[a * BR : (a + 1) * BR]
    total = gathered(a_y, a2[py], ay)
    for a in range(ZL):
        zf[a, 0:AR] = total[a * AR : (a + 1) * AR]
    zs[...] = zf[...].astype(BF16)
    along_z = []
    for d in range(1, NZ):
        target = (pz + d) % NZ
        along_z.append(send(zs.at[target % ZL], zr.at[d], sz.at[d - 1], qz.at[d - 1], at(z=target)))
    zc[0] = gathered(c_y, c3[py], cy).astype(BF16)
    for d in range(1, ZH):
        along_z.append(
            send(zc.at[0], zc.at[d], szc.at[d - 1], qzc.at[d - 1], at(z=(pz + ZL * d) % NZ))
        )
    for copy in along_z:
        copy.wait_recv()
    zr[0] = zs[zl]
    scale = 1.0 / math.sqrt(FRAMES * SHARES * ZH * CORES)
    acc = jnp.zeros((32, 128), F32)
    for z in range(NZ):
        acc = acc + zr[(pz + NZ - z) % NZ].astype(F32)
    fin[core, 0:32] = acc * scale
    acc = jnp.zeros((CR, 128), F32)
    for z in range(ZH):
        acc = acc + zc[(zh + ZH - z) % ZH].astype(F32)
    fin[core, 32:40] = acc * scale
    send(fin.at[core], fin.at[core], s4, q4, partner).wait_recv()

    fin_out[...] = fin[...]
    for copy in sent:
        copy.wait_send()


def finish(scores_in, fgrad_in, fin, scores, fgrad, sq_out, g1_out, g2_out, g3_out, gf_out):
    scores[...] = scores_in[...]
    fgrad[...] = fgrad_in[...]
    g3_out[...] = jnp.concatenate([fin[0, 0:20], fin[1, 0:20]], axis=1)
    for h in range(CORES):
        g2_out[0:CR, h * 128 : (h + 1) * 128] = fin[h, 32:40]
        g2_out[CR:SECOND, h * 128 : (h + 1) * 128] = fin[h, 26:28]
    g1_out[...] = fin[1, 20:25]
    gf_out[...] = fin[1, 25:26].reshape(128)[: (PK * C2) // SHARES]
    for j in range(6):
        sq_out[:, j * 128 : (j + 1) * 128] = fin[0, 20 + j : 21 + j]


def shards(features, cotangent, wp, ws, w1, w2, w3, wf):
    vmem = pl.BlockSpec(memory_space=pltpu.VMEM)
    operands = (features, cotangent, wp, ws, w1, w2, w3, wf.reshape(6, 128))
    dma = pltpu.SemaphoreType.DMA
    outs = pl.pallas_call(
        kernel,
        out_shape=(
            jax.ShapeDtypeStruct((1, FRAMES), F32),
            jax.ShapeDtypeStruct((1, FRAMES, 512), F32),
            jax.ShapeDtypeStruct((2, 40, 128), F32),
        ),
        in_specs=[pl.BlockSpec(memory_space=pltpu.HBM)] * 8,
        out_specs=(vmem,) * 3,
        scratch_shapes=[
            pltpu.VMEM((FRAMES, 512), BF16),
            pltpu.VMEM((1, FRAMES), F32),
            pltpu.VMEM((512, 768), BF16),
            pltpu.VMEM((C0, 768), BF16),
            pltpu.VMEM((HK * C0, C1), BF16),
            pltpu.VMEM((HK * C1, C2), BF16),
            pltpu.VMEM((HK * C2, C2), BF16),
            pltpu.VMEM((6, 128), BF16),
            dma((8,)),
            pltpu.VMEM((2, HALO, 512), BF16),
            pltpu.VMEM((2, 1, FRAMES), F32),
            pltpu.VMEM((FRAMES, (HK + 1) * C0), BF16),
            pltpu.VMEM((FRAMES, HK * C1), BF16),
            pltpu.VMEM((FRAMES, HK * C2), BF16),
            pltpu.VMEM((24, 2 * FRAMES), F32),
            pltpu.VMEM((16, C2), F32),
            pltpu.VMEM((2, HK * C2, 128), F32),
            pltpu.VMEM((2, HK * C1, 128), F32),
            pltpu.VMEM(((HK + 1) * C0, 128), F32),
            pltpu.VMEM((2, SHARES * AR, 128), F32),
            pltpu.VMEM((2, SHARES * CR, 128), F32),
            pltpu.VMEM((2, SHARES * BR, 128), F32),
            pltpu.VMEM((2, NX, NY * ZL * AR, 128), BF16),
            pltpu.VMEM((NX, NY * ZL * AR, 128), BF16),
            pltpu.VMEM((NX, NY * ZL * AR, 128), BF16),
            pltpu.VMEM((NX - 1, NY * ZL * AR, 128), BF16),
            pltpu.VMEM((NY, ZL * AR, 128), BF16),
            pltpu.VMEM((NY - 1, ZL * AR, 128), BF16),
            pltpu.VMEM((2, ZL, NX, NY * CR, 128), BF16),
            pltpu.VMEM((ZL, NX, NY * CR, 128), BF16),
            pltpu.VMEM((ZL, NX, NY * CR, 128), BF16),
            pltpu.VMEM((NX, NY * CR, 128), BF16),
            pltpu.VMEM((NX, NY * CR, 128), BF16),
            pltpu.VMEM((NX - 1, NY * CR, 128), BF16),
            pltpu.VMEM((NY, CR, 128), BF16),
            pltpu.VMEM((NY - 1, CR, 128), BF16),
            pltpu.VMEM((2, NY, NX * ZL * BR, 128), BF16),
            pltpu.VMEM((NY, NX * ZL * BR, 128), BF16),
            pltpu.VMEM((NY, NX * ZL * BR, 128), BF16),
            pltpu.VMEM((NY - 1, NX * ZL * BR, 128), BF16),
            pltpu.VMEM((NX, ZL * BR, 128), BF16),
            pltpu.VMEM((NX - 1, ZL * BR, 128), BF16),
            pltpu.VMEM((ZL, 32, 128), F32),
            pltpu.VMEM((ZL, 32, 128), BF16),
            pltpu.VMEM((NZ, 32, 128), BF16),
            pltpu.VMEM((ZH, CR, 128), BF16),
            pltpu.VMEM((2, 40, 128), F32),
            dma((4,)), dma((4,)),
            dma((3,)), dma((3,)),
            dma((NX - 1,)), dma((NX - 1,)),
            dma((NY - 1,)), dma((NY - 1,)),
            dma, dma,
            dma((NX - 1,)), dma((NX - 1,)),
            dma((NY - 1,)), dma((NY - 1,)),
            dma((NY - 1,)), dma((NY - 1,)),
            dma((NX - 1,)), dma((NX - 1,)),
            dma((NZ - 1,)), dma((NZ - 1,)),
            dma((ZH - 1,)), dma((ZH - 1,)),
            dma, dma,
            pltpu.SemaphoreType.REGULAR((11,)),
        ],
        compiler_params=pltpu.CompilerParams(collective_id=0, has_side_effects=True, vmem_limit_bytes=24 << 20),
    )(*(pltpu.with_memory_space_constraint(v, pltpu.HBM) for v in operands))
    return pl.pallas_call(
        finish,
        out_shape=(
            jax.ShapeDtypeStruct((1, FRAMES), F32),
            jax.ShapeDtypeStruct((1, FRAMES, 512), F32),
            jax.ShapeDtypeStruct((1, 768), F32),
            jax.ShapeDtypeStruct((5, 128), F32),
            jax.ShapeDtypeStruct((10, 256), F32),
            jax.ShapeDtypeStruct((20, 256), F32),
            jax.ShapeDtypeStruct(((PK * C2) // SHARES,), F32),
        ),
        in_specs=[vmem] * 3,
        out_specs=(vmem,) * 7,
        compiler_params=pltpu.CompilerParams(vmem_limit_bytes=4 << 20),
    )(*outs)


def solution(mesh):
    placed = (P("dp", "seq", None), P("dp", "seq"), P(), P(), P(), P(), P(), P())
    return jax.shard_map(
        shards,
        mesh=mesh,
        in_specs=placed,
        out_specs=(
            P("dp", "seq"),
            P("dp", "seq", None),
            P("seq", None),
            P("seq", None),
            P("seq", None),
            P("seq", None),
            P("seq"),
        ),
        check_vma=False,
    )
```

```python
import math

import jax
import jax.numpy as jnp
from jax import lax
from jax.experimental import pallas as pl
from jax.experimental.pallas import tpu as pltpu
from jax.sharding import PartitionSpec as P

MESH = pl.DeviceIdType.MESH
F32 = jnp.float32
BF16 = jnp.bfloat16

C0, C1, C2 = 64, 128, 256
HK, PK = 5, 3
EPSILON = 1e-05
SLOPE = 0.1
FRAMES = 128
HALO = 16
ROWS = FRAMES + 2 * HALO
OWN = slice(HALO, HALO + FRAMES)

ZH, CORES, ZL, NX, NY = 4, 2, 2, 4, 8
NZ = ZH * ZL
SHARES = ZL * NX * NY
AR, CR, BR = 20, 8, 8
SECOND = 10


def dot(a, b, ca=1, cb=0):
    return lax.dot_general(a, b, (((ca,), (cb,)), ((), ())), preferred_element_type=F32)


def normalize(values):
    average = jnp.mean(values, axis=-1, keepdims=True)
    centred = values - average
    variance = jnp.mean(centred * centred, axis=-1, keepdims=True)
    inverse = lax.rsqrt(variance + EPSILON)
    return centred * inverse, inverse


def normalize_back(upstream, normed, inverse):
    first_mean = jnp.mean(upstream, axis=-1, keepdims=True)
    second_mean = jnp.mean(upstream * normed, axis=-1, keepdims=True)
    return (upstream - first_mean - normed * second_mean) * inverse


def activation(v):
    cumulative = 0.5 * (1.0 + lax.erf(v * math.sqrt(0.5)))
    density = jnp.exp(-0.5 * v * v) * (1.0 / math.sqrt(2.0 * math.pi))
    value = SLOPE * v + (1.0 - SLOPE) * (v * cumulative)
    slope = SLOPE + (1.0 - SLOPE) * (cumulative + v * density)
    return value, slope


def shifted(v, shift):
    return pltpu.roll(v, (-shift) % v.shape[0], 0) if shift else v


def split3(v):
    hi = v.astype(BF16).astype(F32)
    mid = (v - hi).astype(BF16).astype(F32)
    return hi, mid, (v - hi - mid).astype(BF16).astype(F32)


def kernel(
    feat_in, cot_in, wp_in, ws_in, w1_in, w2_in, w3_in, wf_in,
    scores, fgrad, fin_out,
    feat, cot, wp, ws, w1, w2, w3, wf, in_sem,
    hfeat, hcot, x1, x2, x3, cots, wfs, g3s, g2s, g1s, ast, cst, bst,
    ab, a0, a1, ax, a2, ay, cb, c0, c1, cz, c2, cx, c3, cy, bb, b0, b1, by, b2, bx,
    zf, zs, zr, zc, fin,
    hs, hr, s0, q0, sax, qax, say, qay, scz, qcz, scx, qcx, scy, qcy, sby, qby, sbx, qbx, sz, qz, szc, qzc, s4, q4, relay,
):
    dp, sq = lax.axis_index("dp"), lax.axis_index("seq")
    zh, core = dp // CORES, dp % CORES
    zl, px, py = sq // (NX * NY), (sq // NY) % NX, sq % NY
    pz = zh * ZL + zl
    count = SHARES

    def at(z=None, x=None, y=None, c=None):
        z = pz if z is None else z
        x = px if x is None else x
        y = py if y is None else y
        c = core if c is None else c
        return ((z // ZL) * CORES + c, (z % ZL) * NX * NY + x * NY + y)

    partner = at(c=1 - core)
    has_low, has_high = sq > 0, sq < count - 1
    before = (jnp.where(has_low, dp, partner[0]), jnp.where(has_low, sq - 1, sq))
    after = (jnp.where(has_high, dp, partner[0]), jnp.where(has_high, sq + 1, sq))
    slot_before, slot_after = jnp.where(has_low, 1, 0), jnp.where(has_high, 0, 1)
    x_up, x_down = at(x=(px + 1) % NX), at(x=(px + NX - 1) % NX)
    y_up, y_down = at(y=(py + 1) % NY), at(y=(py + NY - 1) % NY)
    z_up, z_down = at(z=(pz + 1) % NZ), at(z=(pz + NZ - 1) % NZ)
    peers = [before, after, partner, x_up, x_down, y_up, y_down, z_up, z_down]

    barrier = pltpu.get_barrier_semaphore()
    for peer in peers:
        pl.semaphore_signal(barrier, inc=1, device_id=peer, device_id_type=MESH)
    sources = (feat_in.at[0], cot_in, wp_in, ws_in, w1_in, w2_in, w3_in, wf_in)
    loads = [
        pltpu.make_async_copy(source, target, in_sem.at[i])
        for i, (source, target) in enumerate(zip(sources, (feat, cot, wp, ws, w1, w2, w3, wf)))
    ]
    for load in loads:
        load.start()
    pl.semaphore_wait(barrier, len(peers))

    def send(src, dst, ss, rs, peer):
        copy = pltpu.make_async_remote_copy(
            src_ref=src, dst_ref=dst, send_sem=ss, recv_sem=rs, device_id=peer, device_id_type=MESH
        )
        copy.start()
        sent.append(copy)
        return copy

    sent = []

    loads[0].wait()
    loads[1].wait()
    halo = [
        send(feat.at[pl.ds(FRAMES - HALO, HALO)], hfeat.at[slot_after], hs.at[0], hr.at[slot_after], after),
        send(feat.at[pl.ds(0, HALO)], hfeat.at[slot_before], hs.at[1], hr.at[slot_before], before),
        send(cot, hcot.at[slot_after], hs.at[2], hr.at[2 + slot_after], after),
        send(cot, hcot.at[slot_before], hs.at[3], hr.at[2 + slot_before], before),
    ]

    def tell(*signals):
        for i, peer in signals:
            pl.semaphore_signal(relay.at[i], inc=1, device_id=peer, device_id_type=MESH)

    def hear(*indices):
        for i in indices:
            pl.semaphore_wait(relay.at[i], 1)

    tell((0, x_up), (1, y_up), (2, y_down), (3, z_up), (4, z_down))

    def front(rounded):
        projected = dot(rounded, wp[...]).astype(BF16)
        normed, inverse = normalize(projected.astype(F32))
        rounded = normed.astype(BF16)
        return normed, inverse, rounded, dot(rounded, ws[...], 1, 1)

    def chain(v1, masked):
        taps = [shifted(v1, k - 2).astype(BF16) for k in range(HK)] + [jnp.zeros(v1.shape, BF16)]
        t1 = jnp.concatenate(taps, axis=1)
        v2, slope1 = activation(dot(t1[:, : HK * C0], w1[...]))
        v2 = masked(v2)
        t2 = jnp.concatenate([shifted(v2, k - 2).astype(BF16) for k in range(HK)], axis=1)
        v3, slope2 = activation(dot(t2, w2[...]))
        v3 = masked(v3)
        t3 = jnp.concatenate([shifted(v3, k - 2).astype(BF16) for k in range(HK)], axis=1)
        v4, slope3 = activation(dot(t3, w3[...]))
        return (t1, t2, t3), (slope1, slope2, slope3, masked(v4))

    normed_in, inverse_in = normalize(feat[...].astype(F32))
    loads[2].wait()
    loads[3].wait()
    hidden_normed, hidden_inverse, hidden, squeezed = front(normed_in.astype(BF16))
    v1, squeezed_slope = activation(squeezed)
    for i in (4, 5, 6, 7):
        loads[i].wait()
    own_taps, own_rows = chain(v1, lambda v: v)
    for target, value in zip((x1, x2, x3), own_taps):
        target[...] = value
    for i in range(2):
        for source, target, sem in ((feat.at[pl.ds(0, HALO)], hfeat.at[i], i), (cot, hcot.at[i], 2 + i)):
            pltpu.make_async_remote_copy(
                src_ref=source,
                dst_ref=target,
                send_sem=hs.at[sem],
                recv_sem=hr.at[sem],
                device_id=after,
                device_id_type=MESH,
            ).wait_recv()
    hear(0, 1, 2, 3, 4)
    tell((5, y_up), (6, y_down), (7, z_up), (8, z_down))
    wrow = [
        jnp.concatenate([wf[2 * k : 2 * k + 1, :], wf[2 * k + 1 : 2 * k + 2, :]], axis=1) for k in range(PK)
    ]
    low = jnp.where(has_low, hcot[0], 0.0)
    high = jnp.where(has_high, hcot[1], 0.0)
    line = jnp.concatenate([low, cot[...], high], axis=1)
    cots[...] = jnp.zeros_like(cots)
    wfs[...] = jnp.zeros_like(wfs)
    pieces = split3(line)
    for p in range(3):
        for k in range(PK):
            start = FRAMES - HALO - k + 1
            cots[3 * k + p : 3 * k + p + 1, :] = pltpu.roll(pieces[p], 3 * FRAMES - start, 1)[:, : 2 * FRAMES]
            wfs[3 * k + p : 3 * k + p + 1, :] = wrow[k].astype(F32)
        cots[16 + p : 17 + p, 0:FRAMES] = pieces[p][:, FRAMES : 2 * FRAMES]
    upstream = dot(cots[0:16].astype(BF16), wfs[...].astype(BF16), 0, 0)[:ROWS]
    edge = jnp.concatenate(
        [
            jnp.where(has_low, hfeat[0].astype(F32), 0.0),
            jnp.where(has_high, hfeat[1].astype(F32), 0.0),
        ],
        axis=0,
    )
    edge = activation(front(normalize(edge)[0].astype(BF16))[3])[0]
    edge = jnp.concatenate([edge[:HALO], v1[:HALO], v1[FRAMES - HALO :], edge[HALO:]], axis=0)
    row = lax.broadcasted_iota(jnp.int32, (4 * HALO, 1), 0)
    inside = jnp.logical_and(row >= jnp.where(has_low, 0, HALO), row < jnp.where(has_high, 4 * HALO, 3 * HALO))
    edge_taps, edge_rows = chain(edge, lambda v: jnp.where(inside, v, 0.0))
    for target, value in zip((x1, x2, x3), edge_taps):
        target[0:8] = value[HALO : HALO + 8]
        target[FRAMES - 8 : FRAMES] = value[3 * HALO - 8 : 3 * HALO]
    slope1, slope2, slope3, v4 = (
        jnp.concatenate([strip[: HALO + 8], mid[8 : FRAMES - 8], strip[3 * HALO - 8 :]], axis=0)
        for strip, mid in zip(edge_rows, own_rows)
    )
    row = lax.broadcasted_iota(jnp.int32, (ROWS, 1), 0)
    first_row = jnp.where(has_low, 0, HALO)
    last_row = jnp.where(has_high, ROWS, HALO + FRAMES)
    inside_all = jnp.logical_and(row >= first_row, row < last_row)

    def masked(v):
        return jnp.where(inside_all, v, 0.0)

    delta = masked(upstream * slope3).astype(BF16)
    grad = dot(x3[...], delta[OWN], 0, 0)
    g3s[0], g3s[1] = grad[:, :128], grad[:, 128:]
    plane = NX * NY
    halves = (1 - core, core)
    for h in halves:
        for a in range(ZL):
            for r in range(AR):
                ast.at[h][pl.ds(a * AR + r, plane, stride=ZL * AR), :] = g3s.at[h][
                    pl.ds(a * plane * AR + r, plane, stride=AR), :
                ]
        for x in range(NX):
            ab[h, x] = ast[h, x * NY * ZL * AR : (x + 1) * NY * ZL * AR].astype(BF16)
        if h is halves[0]:
            core_a = send(ab.at[h], a0, s0.at[0], q0.at[0], partner)

    hear(5, 6, 7, 8)
    tell((9, y_up), (10, z_up))

    def back(delta, weight, width):
        d = delta.astype(F32)
        return sum(
            dot(shifted(d, 2 - k).astype(BF16), weight[k * width : (k + 1) * width], 1, 1)
            for k in range(HK)
        )

    def back_narrow(delta, weight, width):
        wide = dot(delta, weight[...], 1, 1)
        return sum(shifted(wide[:, k * width : (k + 1) * width], 2 - k) for k in range(HK))

    upstream = back(delta, w3, C2)
    delta = masked(upstream * slope2).astype(BF16)
    grad = dot(x2[...], delta[OWN], 0, 0)
    g2s[0], g2s[1] = grad[:, :128], grad[:, 128:]
    for h in range(CORES):
        for r in range(CR):
            cst.at[h][pl.ds(r, SHARES, stride=CR), :] = g2s.at[h][pl.ds(r, SHARES, stride=SECOND), :]
        cb[h] = cst[h].astype(BF16).reshape(ZL, NX, NY * CR, 128)
    core_c = send(cb.at[1 - core], c0, s0.at[1], q0.at[1], partner)

    final_taps = [shifted(v4, k - 1)[OWN].astype(BF16) for k in range(PK)]
    total = sum(dot(jnp.broadcast_to(wrow[k], (8, C2)), final_taps[k], 1, 1) for k in range(PK))
    scores[...] = total[0:1]


    own_cot = cots[16:24, 0:FRAMES].astype(BF16)
    final_grad = [
        jnp.sum(dot(own_cot, final_taps[k]), axis=0, keepdims=True) for k in range(PK)
    ]

    upstream = back_narrow(delta, w2, C1)
    delta = masked(upstream * slope1).astype(BF16)
    g1s[...] = dot(x1[...], delta[OWN], 0, 0)
    lines = [(a * plane + x * NY, (x * ZL + a) * BR) for a in range(ZL) for x in range(NX)]
    step = NX * ZL * BR
    for h in range(CORES):
        for share, row in lines:
            for r in range(CR, SECOND):
                bst.at[h][pl.ds(row + r - 2, NY, stride=step), :] = g2s.at[h][
                    pl.ds(SECOND * share + r, NY, stride=SECOND), :
                ]
    for share, row in lines:
        for r in range(5):
            bst.at[1][pl.ds(row + r, NY, stride=step), :] = g1s[pl.ds(5 * share + r, NY, stride=5), :]

    flat = jnp.concatenate(final_grad, axis=1)
    width = (PK * C2) // SHARES
    offset = lax.broadcasted_iota(jnp.int32, (SHARES, PK * C2), 1) - width * lax.broadcasted_iota(
        jnp.int32, (SHARES, PK * C2), 0
    )
    picked = jnp.where(jnp.logical_and(offset >= 0, offset < width), flat, 0.0).astype(BF16)
    place = lax.broadcasted_iota(jnp.int32, (PK * C2, 128), 0)
    place = place - width * ((place * 5462) >> 16) - lax.broadcasted_iota(jnp.int32, (PK * C2, 128), 1)
    spread = jnp.where(place == 0, 1.0, 0.0).astype(BF16)
    spread = dot(picked, spread)
    for share, row in lines:
        bst.at[1][pl.ds(row + 5, NY, stride=step), :] = spread[share : share + NY]

    upstream = back_narrow(delta, w1, C0)
    delta_squeeze = (upstream[OWN] * squeezed_slope).astype(BF16)
    grad = dot(delta_squeeze, hidden, 0, 0)
    for share, row in lines:
        for j in range(6):
            bst.at[0][pl.ds(row + j, NY, stride=step), :] = grad[share : share + NY, j * 128 : (j + 1) * 128]
    for h in range(CORES):
        for y in range(NY):
            bb[h, y] = bst[h, y * step : (y + 1) * step].astype(BF16)
    core_b = send(bb.at[1 - core], b0, s0.at[2], q0.at[2], partner)

    def along_x(source, target, ss, rs):
        return [
            send(source.at[(px + d) % NX], target.at[d - 1], ss.at[d - 1], rs.at[d - 1], at(x=(px + d) % NX))
            for d in range(1, NX)
        ]

    def along_y(source, target, ss, rs):
        return [
            send(source.at[(py + d) % NY], target.at[d - 1], ss.at[d - 1], rs.at[d - 1], at(y=(py + d) % NY))
            for d in range(1, NY)
        ]

    def gathered(copies, own, arrived):
        for copy in copies:
            copy.wait_recv()
        acc = own.astype(F32)
        for d in range(len(copies)):
            acc = acc + arrived[d].astype(F32)
        return acc

    core_a.wait_recv()
    a1[...] = (ab[core].astype(F32) + a0[...].astype(F32)).astype(BF16)
    a_x = along_x(a1, ax, sax, qax)
    core_c.wait_recv()
    c1[...] = (cb[core].astype(F32) + c0[...].astype(F32)).astype(BF16)
    pair = pz + 1 - 2 * zl
    c_z = send(c1.at[1 - zl], cz, scz, qcz, at(z=pair))
    hear(9, 10)
    core_b.wait_recv()
    b1[...] = (bb[core].astype(F32) + b0[...].astype(F32)).astype(BF16)
    b_y = along_y(b1, by, sby, qby)

    hidden_upstream = dot(delta_squeeze, ws[...])
    projected_grad = normalize_back(hidden_upstream, hidden_normed, hidden_inverse).astype(BF16)
    normed_grad = dot(projected_grad, wp[...], 1, 1)
    fgrad[0] = normalize_back(normed_grad, normed_in, inverse_in)

    c_z.wait_recv()
    c2[...] = (c1[zl].astype(F32) + cz[...].astype(F32)).astype(BF16)
    c_x = along_x(c2, cx, scx, qcx)
    a2[...] = gathered(a_x, a1[px], ax).astype(BF16).reshape(NY, ZL * AR, 128)
    a_y = along_y(a2, ay, say, qay)
    c3[...] = gathered(c_x, c2[px], cx).astype(BF16).reshape(NY, CR, 128)
    c_y = along_y(c3, cy, scy, qcy)
    b2[...] = gathered(b_y, b1[py], by).astype(BF16).reshape(NX, ZL * BR, 128)
    b_x = along_x(b2, bx, sbx, qbx)

    zf[...] = jnp.zeros_like(zf)
    total = gathered(b_x, b2[px], bx)
    for a in range(ZL):
        zf[a, AR : AR + BR] = total[a * BR : (a + 1) * BR]
    total = gathered(a_y, a2[py], ay)
    for a in range(ZL):
        zf[a, 0:AR] = total[a * AR : (a + 1) * AR]
    zs[...] = zf[...].astype(BF16)
    along_z = []
    for d in range(1, NZ):
        target = (pz + d) % NZ
        along_z.append(send(zs.at[target % ZL], zr.at[d], sz.at[d - 1], qz.at[d - 1], at(z=target)))
    zc[0] = gathered(c_y, c3[py], cy).astype(BF16)
    for d in range(1, ZH):
        along_z.append(
            send(zc.at[0], zc.at[d], szc.at[d - 1], qzc.at[d - 1], at(z=(pz + ZL * d) % NZ))
        )
    for copy in along_z:
        copy.wait_recv()
    zr[0] = zs[zl]
    scale = 1.0 / math.sqrt(FRAMES * SHARES * ZH * CORES)
    acc = jnp.zeros((32, 128), F32)
    for z in range(NZ):
        acc = acc + zr[(pz + NZ - z) % NZ].astype(F32)
    fin[core, 0:32] = acc * scale
    acc = jnp.zeros((CR, 128), F32)
    for z in range(ZH):
        acc = acc + zc[(zh + ZH - z) % ZH].astype(F32)
    fin[core, 32:40] = acc * scale
    send(fin.at[core], fin.at[core], s4, q4, partner).wait_recv()

    fin_out[...] = fin[...]
    for copy in sent:
        copy.wait_send()


def finish(scores_in, fgrad_in, fin, scores, fgrad, sq_out, g1_out, g2_out, g3_out, gf_out):
    scores[...] = scores_in[...]
    fgrad[...] = fgrad_in[...]
    g3_out[...] = jnp.concatenate([fin[0, 0:20], fin[1, 0:20]], axis=1)
    for h in range(CORES):
        g2_out[0:CR, h * 128 : (h + 1) * 128] = fin[h, 32:40]
        g2_out[CR:SECOND, h * 128 : (h + 1) * 128] = fin[h, 26:28]
    g1_out[...] = fin[1, 20:25]
    gf_out[...] = fin[1, 25:26].reshape(128)[: (PK * C2) // SHARES]
    for j in range(6):
        sq_out[:, j * 128 : (j + 1) * 128] = fin[0, 20 + j : 21 + j]


def shards(features, cotangent, wp, ws, w1, w2, w3, wf):
    vmem = pl.BlockSpec(memory_space=pltpu.VMEM)
    operands = (features, cotangent, wp, ws, w1, w2, w3, wf.reshape(6, 128))
    dma = pltpu.SemaphoreType.DMA
    outs = pl.pallas_call(
        kernel,
        out_shape=(
            jax.ShapeDtypeStruct((1, FRAMES), F32),
            jax.ShapeDtypeStruct((1, FRAMES, 512), F32),
            jax.ShapeDtypeStruct((2, 40, 128), F32),
        ),
        in_specs=[pl.BlockSpec(memory_space=pltpu.HBM)] * 8,
        out_specs=(vmem,) * 3,
        scratch_shapes=[
            pltpu.VMEM((FRAMES, 512), BF16),
            pltpu.VMEM((1, FRAMES), F32),
            pltpu.VMEM((512, 768), BF16),
            pltpu.VMEM((C0, 768), BF16),
            pltpu.VMEM((HK * C0, C1), BF16),
            pltpu.VMEM((HK * C1, C2), BF16),
            pltpu.VMEM((HK * C2, C2), BF16),
            pltpu.VMEM((6, 128), BF16),
            dma((8,)),
            pltpu.VMEM((2, HALO, 512), BF16),
            pltpu.VMEM((2, 1, FRAMES), F32),
            pltpu.VMEM((FRAMES, (HK + 1) * C0), BF16),
            pltpu.VMEM((FRAMES, HK * C1), BF16),
            pltpu.VMEM((FRAMES, HK * C2), BF16),
            pltpu.VMEM((24, 2 * FRAMES), F32),
            pltpu.VMEM((16, C2), F32),
            pltpu.VMEM((2, HK * C2, 128), F32),
            pltpu.VMEM((2, HK * C1, 128), F32),
            pltpu.VMEM(((HK + 1) * C0, 128), F32),
            pltpu.VMEM((2, SHARES * AR, 128), F32),
            pltpu.VMEM((2, SHARES * CR, 128), F32),
            pltpu.VMEM((2, SHARES * BR, 128), F32),
            pltpu.VMEM((2, NX, NY * ZL * AR, 128), BF16),
            pltpu.VMEM((NX, NY * ZL * AR, 128), BF16),
            pltpu.VMEM((NX, NY * ZL * AR, 128), BF16),
            pltpu.VMEM((NX - 1, NY * ZL * AR, 128), BF16),
            pltpu.VMEM((NY, ZL * AR, 128), BF16),
            pltpu.VMEM((NY - 1, ZL * AR, 128), BF16),
            pltpu.VMEM((2, ZL, NX, NY * CR, 128), BF16),
            pltpu.VMEM((ZL, NX, NY * CR, 128), BF16),
            pltpu.VMEM((ZL, NX, NY * CR, 128), BF16),
            pltpu.VMEM((NX, NY * CR, 128), BF16),
            pltpu.VMEM((NX, NY * CR, 128), BF16),
            pltpu.VMEM((NX - 1, NY * CR, 128), BF16),
            pltpu.VMEM((NY, CR, 128), BF16),
            pltpu.VMEM((NY - 1, CR, 128), BF16),
            pltpu.VMEM((2, NY, NX * ZL * BR, 128), BF16),
            pltpu.VMEM((NY, NX * ZL * BR, 128), BF16),
            pltpu.VMEM((NY, NX * ZL * BR, 128), BF16),
            pltpu.VMEM((NY - 1, NX * ZL * BR, 128), BF16),
            pltpu.VMEM((NX, ZL * BR, 128), BF16),
            pltpu.VMEM((NX - 1, ZL * BR, 128), BF16),
            pltpu.VMEM((ZL, 32, 128), F32),
            pltpu.VMEM((ZL, 32, 128), BF16),
            pltpu.VMEM((NZ, 32, 128), BF16),
            pltpu.VMEM((ZH, CR, 128), BF16),
            pltpu.VMEM((2, 40, 128), F32),
            dma((4,)), dma((4,)),
            dma((3,)), dma((3,)),
            dma((NX - 1,)), dma((NX - 1,)),
            dma((NY - 1,)), dma((NY - 1,)),
            dma, dma,
            dma((NX - 1,)), dma((NX - 1,)),
            dma((NY - 1,)), dma((NY - 1,)),
            dma((NY - 1,)), dma((NY - 1,)),
            dma((NX - 1,)), dma((NX - 1,)),
            dma((NZ - 1,)), dma((NZ - 1,)),
            dma((ZH - 1,)), dma((ZH - 1,)),
            dma, dma,
            pltpu.SemaphoreType.REGULAR((11,)),
        ],
        compiler_params=pltpu.CompilerParams(collective_id=0, has_side_effects=True, vmem_limit_bytes=24 << 20),
    )(*(pltpu.with_memory_space_constraint(v, pltpu.HBM) for v in operands))
    return pl.pallas_call(
        finish,
        out_shape=(
            jax.ShapeDtypeStruct((1, FRAMES), F32),
            jax.ShapeDtypeStruct((1, FRAMES, 512), F32),
            jax.ShapeDtypeStruct((1, 768), F32),
            jax.ShapeDtypeStruct((5, 128), F32),
            jax.ShapeDtypeStruct((10, 256), F32),
            jax.ShapeDtypeStruct((20, 256), F32),
            jax.ShapeDtypeStruct(((PK * C2) // SHARES,), F32),
        ),
        in_specs=[vmem] * 3,
        out_specs=(vmem,) * 7,
        compiler_params=pltpu.CompilerParams(vmem_limit_bytes=4 << 20),
    )(*outs)


def solution(mesh):
    placed = (P("dp", "seq", None), P("dp", "seq"), P(), P(), P(), P(), P(), P())
    return jax.shard_map(
        shards,
        mesh=mesh,
        in_specs=placed,
        out_specs=(
            P("dp", "seq"),
            P("dp", "seq", None),
            P("seq", None),
            P("seq", None),
            P("seq", None),
            P("seq", None),
            P("seq"),
        ),
        check_vma=False,
    )
```

```python
import math

import jax
import jax.numpy as jnp
from jax import lax
from jax.experimental import pallas as pl
from jax.experimental.pallas import tpu as pltpu
from jax.sharding import PartitionSpec as P

MESH = pl.DeviceIdType.MESH
F32 = jnp.float32
BF16 = jnp.bfloat16

C0, C1, C2 = 64, 128, 256
HK, PK = 5, 3
EPSILON = 1e-05
SLOPE = 0.1
FRAMES = 128
HALO = 16
ROWS = FRAMES + 2 * HALO
OWN = slice(HALO, HALO + FRAMES)

ZH, CORES, ZL, NX, NY = 4, 2, 2, 4, 8
NZ = ZH * ZL
SHARES = ZL * NX * NY
AR, CR, BR = 20, 8, 8
SECOND = 10


def dot(a, b, ca=1, cb=0):
    return lax.dot_general(a, b, (((ca,), (cb,)), ((), ())), preferred_element_type=F32)


def normalize(values):
    average = jnp.mean(values, axis=-1, keepdims=True)
    centred = values - average
    variance = jnp.mean(centred * centred, axis=-1, keepdims=True)
    inverse = lax.rsqrt(variance + EPSILON)
    return centred * inverse, inverse


def normalize_back(upstream, normed, inverse):
    first_mean = jnp.mean(upstream, axis=-1, keepdims=True)
    second_mean = jnp.mean(upstream * normed, axis=-1, keepdims=True)
    return (upstream - first_mean - normed * second_mean) * inverse


def activation(v):
    cumulative = 0.5 * (1.0 + lax.erf(v * math.sqrt(0.5)))
    density = jnp.exp(-0.5 * v * v) * (1.0 / math.sqrt(2.0 * math.pi))
    value = SLOPE * v + (1.0 - SLOPE) * (v * cumulative)
    slope = SLOPE + (1.0 - SLOPE) * (cumulative + v * density)
    return value, slope


def shifted(v, shift):
    return pltpu.roll(v, (-shift) % v.shape[0], 0) if shift else v


def split3(v):
    hi = v.astype(BF16).astype(F32)
    mid = (v - hi).astype(BF16).astype(F32)
    return hi, mid, (v - hi - mid).astype(BF16).astype(F32)


def kernel(
    feat_in, cot_in, wp_in, ws_in, w1_in, w2_in, w3_in, wf_in,
    scores, fgrad_out, fin_out,
    fgrad, out_sem,
    feat, cot, wp, ws, w1, w2, w3, wf, in_sem,
    hfeat, hcot, x1, x2, x3, cots, wfs, g3s, g2s, g1s, ast, cst, bst,
    ab, a0, a1, ax, a2, ay, cb, c0, c1, cz, c2, cx, c3, cy, bb, b0, b1, by, b2, bx,
    zf, zs, zr, zc, fin,
    hs, hr, s0, q0, sax, qax, say, qay, scz, qcz, scx, qcx, scy, qcy, sby, qby, sbx, qbx, sz, qz, szc, qzc, s4, q4, relay,
):
    dp, sq = lax.axis_index("dp"), lax.axis_index("seq")
    zh, core = dp // CORES, dp % CORES
    zl, px, py = sq // (NX * NY), (sq // NY) % NX, sq % NY
    pz = zh * ZL + zl
    count = SHARES

    def at(z=None, x=None, y=None, c=None):
        z = pz if z is None else z
        x = px if x is None else x
        y = py if y is None else y
        c = core if c is None else c
        return ((z // ZL) * CORES + c, (z % ZL) * NX * NY + x * NY + y)

    partner = at(c=1 - core)
    has_low, has_high = sq > 0, sq < count - 1
    before = (jnp.where(has_low, dp, partner[0]), jnp.where(has_low, sq - 1, sq))
    after = (jnp.where(has_high, dp, partner[0]), jnp.where(has_high, sq + 1, sq))
    slot_before, slot_after = jnp.where(has_low, 1, 0), jnp.where(has_high, 0, 1)
    x_up, x_down = at(x=(px + 1) % NX), at(x=(px + NX - 1) % NX)
    y_up, y_down = at(y=(py + 1) % NY), at(y=(py + NY - 1) % NY)
    z_up, z_down = at(z=(pz + 1) % NZ), at(z=(pz + NZ - 1) % NZ)
    peers = [before, after, partner, x_up, x_down, y_up, y_down, z_up, z_down]

    barrier = pltpu.get_barrier_semaphore()
    for peer in peers:
        pl.semaphore_signal(barrier, inc=1, device_id=peer, device_id_type=MESH)
    sources = (feat_in.at[0], cot_in, wp_in, ws_in, w1_in, w2_in, w3_in, wf_in)
    loads = [
        pltpu.make_async_copy(source, target, in_sem.at[i])
        for i, (source, target) in enumerate(zip(sources, (feat, cot, wp, ws, w1, w2, w3, wf)))
    ]
    for load in loads:
        load.start()
    pl.semaphore_wait(barrier, len(peers))

    def send(src, dst, ss, rs, peer):
        copy = pltpu.make_async_remote_copy(
            src_ref=src, dst_ref=dst, send_sem=ss, recv_sem=rs, device_id=peer, device_id_type=MESH
        )
        copy.start()
        sent.append(copy)
        return copy

    sent = []

    loads[0].wait()
    loads[1].wait()
    halo = [
        send(feat.at[pl.ds(FRAMES - HALO, HALO)], hfeat.at[slot_after], hs.at[0], hr.at[slot_after], after),
        send(feat.at[pl.ds(0, HALO)], hfeat.at[slot_before], hs.at[1], hr.at[slot_before], before),
        send(cot, hcot.at[slot_after], hs.at[2], hr.at[2 + slot_after], after),
        send(cot, hcot.at[slot_before], hs.at[3], hr.at[2 + slot_before], before),
    ]

    def tell(*signals):
        for i, peer in signals:
            pl.semaphore_signal(relay.at[i], inc=1, device_id=peer, device_id_type=MESH)

    def hear(*indices):
        for i in indices:
            pl.semaphore_wait(relay.at[i], 1)

    tell((0, x_up), (1, y_up), (2, y_down), (3, z_up), (4, z_down))

    def front(rounded):
        projected = dot(rounded, wp[...]).astype(BF16)
        normed, inverse = normalize(projected.astype(F32))
        rounded = normed.astype(BF16)
        return normed, inverse, rounded, dot(rounded, ws[...], 1, 1)

    def chain(v1, masked):
        taps = [shifted(v1, k - 2).astype(BF16) for k in range(HK)] + [jnp.zeros(v1.shape, BF16)]
        t1 = jnp.concatenate(taps, axis=1)
        v2, slope1 = activation(dot(t1[:, : HK * C0], w1[...]))
        v2 = masked(v2)
        t2 = jnp.concatenate([shifted(v2, k - 2).astype(BF16) for k in range(HK)], axis=1)
        v3, slope2 = activation(dot(t2, w2[...]))
        v3 = masked(v3)
        t3 = jnp.concatenate([shifted(v3, k - 2).astype(BF16) for k in range(HK)], axis=1)
        v4, slope3 = activation(dot(t3, w3[...]))
        return (t1, t2, t3), (slope1, slope2, slope3, masked(v4))

    normed_in, inverse_in = normalize(feat[...].astype(F32))
    loads[2].wait()
    loads[3].wait()
    hidden_normed, hidden_inverse, hidden, squeezed = front(normed_in.astype(BF16))
    v1, squeezed_slope = activation(squeezed)
    for i in (4, 5, 6, 7):
        loads[i].wait()
    own_taps, own_rows = chain(v1, lambda v: v)
    for target, value in zip((x1, x2, x3), own_taps):
        target[...] = value
    for i in range(2):
        for source, target, sem in ((feat.at[pl.ds(0, HALO)], hfeat.at[i], i), (cot, hcot.at[i], 2 + i)):
            pltpu.make_async_remote_copy(
                src_ref=source,
                dst_ref=target,
                send_sem=hs.at[sem],
                recv_sem=hr.at[sem],
                device_id=after,
                device_id_type=MESH,
            ).wait_recv()
    hear(0, 1, 2, 3, 4)
    tell((5, y_up), (6, y_down), (7, z_up), (8, z_down))
    wrow = [
        jnp.concatenate([wf[2 * k : 2 * k + 1, :], wf[2 * k + 1 : 2 * k + 2, :]], axis=1) for k in range(PK)
    ]
    low = jnp.where(has_low, hcot[0], 0.0)
    high = jnp.where(has_high, hcot[1], 0.0)
    line = jnp.concatenate([low, cot[...], high], axis=1)
    cots[...] = jnp.zeros_like(cots)
    wfs[...] = jnp.zeros_like(wfs)
    pieces = split3(line)
    for p in range(3):
        for k in range(PK):
            start = FRAMES - HALO - k + 1
            cots[3 * k + p : 3 * k + p + 1, :] = pltpu.roll(pieces[p], 3 * FRAMES - start, 1)[:, : 2 * FRAMES]
            wfs[3 * k + p : 3 * k + p + 1, :] = wrow[k].astype(F32)
        cots[16 + p : 17 + p, 0:FRAMES] = pieces[p][:, FRAMES : 2 * FRAMES]
    upstream = dot(cots[0:16].astype(BF16), wfs[...].astype(BF16), 0, 0)[:ROWS]
    edge = jnp.concatenate(
        [
            jnp.where(has_low, hfeat[0].astype(F32), 0.0),
            jnp.where(has_high, hfeat[1].astype(F32), 0.0),
        ],
        axis=0,
    )
    edge = activation(front(normalize(edge)[0].astype(BF16))[3])[0]
    edge = jnp.concatenate([edge[:HALO], v1[:HALO], v1[FRAMES - HALO :], edge[HALO:]], axis=0)
    row = lax.broadcasted_iota(jnp.int32, (4 * HALO, 1), 0)
    inside = jnp.logical_and(row >= jnp.where(has_low, 0, HALO), row < jnp.where(has_high, 4 * HALO, 3 * HALO))
    edge_taps, edge_rows = chain(edge, lambda v: jnp.where(inside, v, 0.0))
    for target, value in zip((x1, x2, x3), edge_taps):
        target[0:8] = value[HALO : HALO + 8]
        target[FRAMES - 8 : FRAMES] = value[3 * HALO - 8 : 3 * HALO]
    slope1, slope2, slope3, v4 = (
        jnp.concatenate([strip[: HALO + 8], mid[8 : FRAMES - 8], strip[3 * HALO - 8 :]], axis=0)
        for strip, mid in zip(edge_rows, own_rows)
    )
    row = lax.broadcasted_iota(jnp.int32, (ROWS, 1), 0)
    first_row = jnp.where(has_low, 0, HALO)
    last_row = jnp.where(has_high, ROWS, HALO + FRAMES)
    inside_all = jnp.logical_and(row >= first_row, row < last_row)

    def masked(v):
        return jnp.where(inside_all, v, 0.0)

    delta = masked(upstream * slope3).astype(BF16)
    grad = dot(x3[...], delta[OWN], 0, 0)
    g3s[0], g3s[1] = grad[:, :128], grad[:, 128:]
    plane = NX * NY
    halves = (1 - core, core)
    for h in halves:
        for a in range(ZL):
            for r in range(AR):
                ast.at[h][pl.ds(a * AR + r, plane, stride=ZL * AR), :] = g3s.at[h][
                    pl.ds(a * plane * AR + r, plane, stride=AR), :
                ]
        for x in range(NX):
            ab[h, x] = ast[h, x * NY * ZL * AR : (x + 1) * NY * ZL * AR].astype(BF16)
        if h is halves[0]:
            core_a = send(ab.at[h], a0, s0.at[0], q0.at[0], partner)

    hear(5, 6, 7, 8)
    tell((9, y_up), (10, z_up))

    def back(delta, weight, width):
        d = delta.astype(F32)
        return sum(
            dot(shifted(d, 2 - k).astype(BF16), weight[k * width : (k + 1) * width], 1, 1)
            for k in range(HK)
        )

    def back_narrow(delta, weight, width):
        wide = dot(delta, weight[...], 1, 1)
        return sum(shifted(wide[:, k * width : (k + 1) * width], 2 - k) for k in range(HK))

    upstream = back(delta, w3, C2)
    delta = masked(upstream * slope2).astype(BF16)
    grad = dot(x2[...], delta[OWN], 0, 0)
    g2s[0], g2s[1] = grad[:, :128], grad[:, 128:]
    for h in range(CORES):
        for r in range(CR):
            cst.at[h][pl.ds(r, SHARES, stride=CR), :] = g2s.at[h][pl.ds(r, SHARES, stride=SECOND), :]
        cb[h] = cst[h].astype(BF16).reshape(ZL, NX, NY * CR, 128)
    core_c = send(cb.at[1 - core], c0, s0.at[1], q0.at[1], partner)

    final_taps = [shifted(v4, k - 1)[OWN].astype(BF16) for k in range(PK)]
    total = sum(dot(jnp.broadcast_to(wrow[k], (8, C2)), final_taps[k], 1, 1) for k in range(PK))
    scores[...] = total[0:1]


    own_cot = cots[16:24, 0:FRAMES].astype(BF16)
    final_grad = [
        jnp.sum(dot(own_cot, final_taps[k]), axis=0, keepdims=True) for k in range(PK)
    ]

    upstream = back_narrow(delta, w2, C1)
    delta = masked(upstream * slope1).astype(BF16)
    g1s[...] = dot(x1[...], delta[OWN], 0, 0)
    lines = [(a * plane + x * NY, (x * ZL + a) * BR) for a in range(ZL) for x in range(NX)]
    step = NX * ZL * BR
    for h in range(CORES):
        for share, row in lines:
            for r in range(CR, SECOND):
                bst.at[h][pl.ds(row + r - 2, NY, stride=step), :] = g2s.at[h][
                    pl.ds(SECOND * share + r, NY, stride=SECOND), :
                ]
    for share, row in lines:
        for r in range(5):
            bst.at[1][pl.ds(row + r, NY, stride=step), :] = g1s[pl.ds(5 * share + r, NY, stride=5), :]

    flat = jnp.concatenate(final_grad, axis=1)
    width = (PK * C2) // SHARES
    offset = lax.broadcasted_iota(jnp.int32, (SHARES, PK * C2), 1) - width * lax.broadcasted_iota(
        jnp.int32, (SHARES, PK * C2), 0
    )
    picked = jnp.where(jnp.logical_and(offset >= 0, offset < width), flat, 0.0).astype(BF16)
    place = lax.broadcasted_iota(jnp.int32, (PK * C2, 128), 0)
    place = place - width * ((place * 5462) >> 16) - lax.broadcasted_iota(jnp.int32, (PK * C2, 128), 1)
    spread = jnp.where(place == 0, 1.0, 0.0).astype(BF16)
    spread = dot(picked, spread)
    for share, row in lines:
        bst.at[1][pl.ds(row + 5, NY, stride=step), :] = spread[share : share + NY]

    upstream = back_narrow(delta, w1, C0)
    delta_squeeze = (upstream[OWN] * squeezed_slope).astype(BF16)
    grad = dot(delta_squeeze, hidden, 0, 0)
    for share, row in lines:
        for j in range(6):
            bst.at[0][pl.ds(row + j, NY, stride=step), :] = grad[share : share + NY, j * 128 : (j + 1) * 128]
    for h in range(CORES):
        for y in range(NY):
            bb[h, y] = bst[h, y * step : (y + 1) * step].astype(BF16)
    core_b = send(bb.at[1 - core], b0, s0.at[2], q0.at[2], partner)

    def along_x(source, target, ss, rs):
        return [
            send(source.at[(px + d) % NX], target.at[d - 1], ss.at[d - 1], rs.at[d - 1], at(x=(px + d) % NX))
            for d in range(1, NX)
        ]

    def along_y(source, target, ss, rs):
        return [
            send(source.at[(py + d) % NY], target.at[d - 1], ss.at[d - 1], rs.at[d - 1], at(y=(py + d) % NY))
            for d in range(1, NY)
        ]

    def gathered(copies, own, arrived):
        for copy in copies:
            copy.wait_recv()
        acc = own.astype(F32)
        for d in range(len(copies)):
            acc = acc + arrived[d].astype(F32)
        return acc

    core_a.wait_recv()
    a1[...] = (ab[core].astype(F32) + a0[...].astype(F32)).astype(BF16)
    a_x = along_x(a1, ax, sax, qax)
    core_c.wait_recv()
    c1[...] = (cb[core].astype(F32) + c0[...].astype(F32)).astype(BF16)
    pair = pz + 1 - 2 * zl
    c_z = send(c1.at[1 - zl], cz, scz, qcz, at(z=pair))
    hear(9, 10)
    core_b.wait_recv()
    b1[...] = (bb[core].astype(F32) + b0[...].astype(F32)).astype(BF16)
    b_y = along_y(b1, by, sby, qby)

    hidden_upstream = dot(delta_squeeze, ws[...])
    projected_grad = normalize_back(hidden_upstream, hidden_normed, hidden_inverse).astype(BF16)
    normed_grad = dot(projected_grad, wp[...], 1, 1)
    fgrad[0] = normalize_back(normed_grad, normed_in, inverse_in)
    written = pltpu.make_async_copy(fgrad, fgrad_out, out_sem)
    written.start()

    c_z.wait_recv()
    c2[...] = (c1[zl].astype(F32) + cz[...].astype(F32)).astype(BF16)
    c_x = along_x(c2, cx, scx, qcx)
    a2[...] = gathered(a_x, a1[px], ax).astype(BF16).reshape(NY, ZL * AR, 128)
    a_y = along_y(a2, ay, say, qay)
    c3[...] = gathered(c_x, c2[px], cx).astype(BF16).reshape(NY, CR, 128)
    c_y = along_y(c3, cy, scy, qcy)
    b2[...] = gathered(b_y, b1[py], by).astype(BF16).reshape(NX, ZL * BR, 128)
    b_x = along_x(b2, bx, sbx, qbx)

    zf[...] = jnp.zeros_like(zf)
    total = gathered(b_x, b2[px], bx)
    for a in range(ZL):
        zf[a, AR : AR + BR] = total[a * BR : (a + 1) * BR]
    total = gathered(a_y, a2[py], ay)
    for a in range(ZL):
        zf[a, 0:AR] = total[a * AR : (a + 1) * AR]
    zs[...] = zf[...].astype(BF16)
    along_z = []
    for d in range(1, NZ):
        target = (pz + d) % NZ
        along_z.append(send(zs.at[target % ZL], zr.at[d], sz.at[d - 1], qz.at[d - 1], at(z=target)))
    zc[0] = gathered(c_y, c3[py], cy).astype(BF16)
    for d in range(1, ZH):
        along_z.append(
            send(zc.at[0], zc.at[d], szc.at[d - 1], qzc.at[d - 1], at(z=(pz + ZL * d) % NZ))
        )
    for copy in along_z:
        copy.wait_recv()
    zr[0] = zs[zl]
    scale = 1.0 / math.sqrt(FRAMES * SHARES * ZH * CORES)
    acc = jnp.zeros((32, 128), F32)
    for z in range(NZ):
        acc = acc + zr[(pz + NZ - z) % NZ].astype(F32)
    fin[core, 0:32] = acc * scale
    acc = jnp.zeros((CR, 128), F32)
    for z in range(ZH):
        acc = acc + zc[(zh + ZH - z) % ZH].astype(F32)
    fin[core, 32:40] = acc * scale
    send(fin.at[core], fin.at[core], s4, q4, partner).wait_recv()

    fin_out[...] = fin[...]
    written.wait()
    for copy in sent:
        copy.wait_send()


def finish(scores_in, fgrad_in, fin, scores, fgrad, sq_out, g1_out, g2_out, g3_out, gf_out):
    fgrad[...] = fgrad_in[...]
    scores[...] = scores_in[...]
    g3_out[...] = jnp.concatenate([fin[0, 0:20], fin[1, 0:20]], axis=1)
    for h in range(CORES):
        g2_out[0:CR, h * 128 : (h + 1) * 128] = fin[h, 32:40]
        g2_out[CR:SECOND, h * 128 : (h + 1) * 128] = fin[h, 26:28]
    g1_out[...] = fin[1, 20:25]
    gf_out[...] = fin[1, 25:26].reshape(128)[: (PK * C2) // SHARES]
    for j in range(6):
        sq_out[:, j * 128 : (j + 1) * 128] = fin[0, 20 + j : 21 + j]


def shards(features, cotangent, wp, ws, w1, w2, w3, wf):
    vmem = pl.BlockSpec(memory_space=pltpu.VMEM)
    operands = (features, cotangent, wp, ws, w1, w2, w3, wf.reshape(6, 128))
    dma = pltpu.SemaphoreType.DMA
    outs = pl.pallas_call(
        kernel,
        out_shape=(
            jax.ShapeDtypeStruct((1, FRAMES), F32),
            jax.ShapeDtypeStruct((1, FRAMES, 512), F32),
            jax.ShapeDtypeStruct((2, 40, 128), F32),
        ),
        in_specs=[pl.BlockSpec(memory_space=pltpu.HBM)] * 8,
        out_specs=(vmem, pl.BlockSpec(memory_space=pl.ANY), vmem),
        scratch_shapes=[
            pltpu.VMEM((1, FRAMES, 512), F32),
            dma,
            pltpu.VMEM((FRAMES, 512), BF16),
            pltpu.VMEM((1, FRAMES), F32),
            pltpu.VMEM((512, 768), BF16),
            pltpu.VMEM((C0, 768), BF16),
            pltpu.VMEM((HK * C0, C1), BF16),
            pltpu.VMEM((HK * C1, C2), BF16),
            pltpu.VMEM((HK * C2, C2), BF16),
            pltpu.VMEM((6, 128), BF16),
            dma((8,)),
            pltpu.VMEM((2, HALO, 512), BF16),
            pltpu.VMEM((2, 1, FRAMES), F32),
            pltpu.VMEM((FRAMES, (HK + 1) * C0), BF16),
            pltpu.VMEM((FRAMES, HK * C1), BF16),
            pltpu.VMEM((FRAMES, HK * C2), BF16),
            pltpu.VMEM((24, 2 * FRAMES), F32),
            pltpu.VMEM((16, C2), F32),
            pltpu.VMEM((2, HK * C2, 128), F32),
            pltpu.VMEM((2, HK * C1, 128), F32),
            pltpu.VMEM(((HK + 1) * C0, 128), F32),
            pltpu.VMEM((2, SHARES * AR, 128), F32),
            pltpu.VMEM((2, SHARES * CR, 128), F32),
            pltpu.VMEM((2, SHARES * BR, 128), F32),
            pltpu.VMEM((2, NX, NY * ZL * AR, 128), BF16),
            pltpu.VMEM((NX, NY * ZL * AR, 128), BF16),
            pltpu.VMEM((NX, NY * ZL * AR, 128), BF16),
            pltpu.VMEM((NX - 1, NY * ZL * AR, 128), BF16),
            pltpu.VMEM((NY, ZL * AR, 128), BF16),
            pltpu.VMEM((NY - 1, ZL * AR, 128), BF16),
            pltpu.VMEM((2, ZL, NX, NY * CR, 128), BF16),
            pltpu.VMEM((ZL, NX, NY * CR, 128), BF16),
            pltpu.VMEM((ZL, NX, NY * CR, 128), BF16),
            pltpu.VMEM((NX, NY * CR, 128), BF16),
            pltpu.VMEM((NX, NY * CR, 128), BF16),
            pltpu.VMEM((NX - 1, NY * CR, 128), BF16),
            pltpu.VMEM((NY, CR, 128), BF16),
            pltpu.VMEM((NY - 1, CR, 128), BF16),
            pltpu.VMEM((2, NY, NX * ZL * BR, 128), BF16),
            pltpu.VMEM((NY, NX * ZL * BR, 128), BF16),
            pltpu.VMEM((NY, NX * ZL * BR, 128), BF16),
            pltpu.VMEM((NY - 1, NX * ZL * BR, 128), BF16),
            pltpu.VMEM((NX, ZL * BR, 128), BF16),
            pltpu.VMEM((NX - 1, ZL * BR, 128), BF16),
            pltpu.VMEM((ZL, 32, 128), F32),
            pltpu.VMEM((ZL, 32, 128), BF16),
            pltpu.VMEM((NZ, 32, 128), BF16),
            pltpu.VMEM((ZH, CR, 128), BF16),
            pltpu.VMEM((2, 40, 128), F32),
            dma((4,)), dma((4,)),
            dma((3,)), dma((3,)),
            dma((NX - 1,)), dma((NX - 1,)),
            dma((NY - 1,)), dma((NY - 1,)),
            dma, dma,
            dma((NX - 1,)), dma((NX - 1,)),
            dma((NY - 1,)), dma((NY - 1,)),
            dma((NY - 1,)), dma((NY - 1,)),
            dma((NX - 1,)), dma((NX - 1,)),
            dma((NZ - 1,)), dma((NZ - 1,)),
            dma((ZH - 1,)), dma((ZH - 1,)),
            dma, dma,
            pltpu.SemaphoreType.REGULAR((11,)),
        ],
        compiler_params=pltpu.CompilerParams(collective_id=0, has_side_effects=True, vmem_limit_bytes=24 << 20),
    )(*(pltpu.with_memory_space_constraint(v, pltpu.HBM) for v in operands))
    return pl.pallas_call(
        finish,
        out_shape=(
            jax.ShapeDtypeStruct((1, FRAMES), F32),
            jax.ShapeDtypeStruct((1, FRAMES, 512), F32),
            jax.ShapeDtypeStruct((1, 768), F32),
            jax.ShapeDtypeStruct((5, 128), F32),
            jax.ShapeDtypeStruct((10, 256), F32),
            jax.ShapeDtypeStruct((20, 256), F32),
            jax.ShapeDtypeStruct(((PK * C2) // SHARES,), F32),
        ),
        in_specs=[vmem] * 3,
        out_specs=(vmem,) * 7,
        compiler_params=pltpu.CompilerParams(vmem_limit_bytes=4 << 20),
    )(*outs)


def solution(mesh):
    placed = (P("dp", "seq", None), P("dp", "seq"), P(), P(), P(), P(), P(), P())
    return jax.shard_map(
        shards,
        mesh=mesh,
        in_specs=placed,
        out_specs=(
            P("dp", "seq"),
            P("dp", "seq", None),
            P("seq", None),
            P("seq", None),
            P("seq", None),
            P("seq", None),
            P("seq"),
        ),
        check_vma=False,
    )
```
